128 devices in a mesh: row: 4 (over y), col: 32 (over x, z, core).
Axes of the slice: x: 4, y: 4, z: 4, core: 2. Of those that a mesh axis runs over, the one named last changes fastest.
Arguments:
- left_site: bfloat16 [4096, 2048], P('row', 'col')
- right_site: bfloat16 [2048, 4096], P('row', 'col'), may hold values from -0.125 to 0.125
- gate: float32 [4, 4], replicated, may hold values from -0.6 to 2.1
- omega: bfloat16 [4096, 2304], P(None, 'row'), may hold values from -0.09375 to 0.09375
Outputs:
- basis: float32 [4096, 2304], P(('row', 'col'))
- projected: float32 [2304, 4096], P('row', 'col')
The draws below stay inside these ranges and needn't reach their ends.
All inputs are finite; a program needn't handle non-finite values.
Results may differ from the reference program's by a relative error of at most 0.0085.
Values may be sent and summed in bfloat16 or wider, within the bound.
A program may use at most 192 MiB of HBM per device.

```python
import math
import jax
import jax.numpy as jnp
from jax import lax

CHI = 2048
K = 2304
ROWS = 4096


def draw_left_site(key, part):
    noise_key, rough_key = jax.random.split(jax.random.fold_in(key, 11))
    noise = jnp.clip(jax.random.normal(noise_key, (ROWS, CHI), jnp.float32), -4.0, 4.0)
    top_scale = 3.0
    ramp = jnp.arange(ROWS, dtype=jnp.float32) / ROWS
    rough = jnp.exp(jax.random.uniform(rough_key, (ROWS, 1), jnp.float32, -0.35, 0.35))
    scales = jnp.power(top_scale, ramp)[:, None] * rough
    return (noise * scales).astype(jnp.bfloat16)


def draw_gate(key, part):
    entries = jax.random.uniform(jax.random.fold_in(key, 23), (4, 4), jnp.float32, -0.6, 0.6)
    return entries + 1.5 * jnp.eye(4, dtype=jnp.float32)


def steps_of(own_key, dims, cuts, low, high):
    loudness = 1.0
    for axis_at, parts in cuts:
        draws = jax.random.uniform(jax.random.fold_in(jax.random.fold_in(own_key, 6), axis_at), (parts,), jnp.float32, low / len(cuts), high / len(cuts))
        loudness = loudness * jnp.repeat(jnp.exp(draws), dims[axis_at] // parts).reshape((-1,) + (1,) * (len(dims) - 1 - axis_at))
    return loudness


def centred(own_key, extent, scale, bound, pieces=(), kind=jnp.bfloat16):
    loudness = steps_of(own_key, extent, pieces, -0.22, 0.18) if pieces else 1.0
    drawn = jax.random.normal(own_key, extent, jnp.float32) * scale * loudness
    return jnp.minimum(jnp.maximum(drawn, -bound), bound).astype(kind)


def setup_inputs(seed: int = 0) -> dict:
    keys = jax.random.split(jax.random.key(seed), 5)
    return {
        "left_site": draw_left_site(jax.random.fold_in(keys[4], 71), 0),
        "right_site": centred(keys[1], (CHI, ROWS), CHI ** -0.5, 0.125, ((0, 4), (1, 32))),
        "gate": draw_gate(jax.random.fold_in(keys[4], 71), 0),
        "omega": centred(keys[3], (ROWS, K), ROWS ** -0.5, 0.09375, ((1, 4),)),
    }


def reference(left_site, right_site, gate, omega):
    bare = jnp.dot(left_site.astype(jnp.float32), right_site.astype(jnp.float32), preferred_element_type=jnp.float32)
    quad = bare.reshape(CHI, 2, CHI, 2)
    gate_four = gate.astype(jnp.float32).reshape(2, 2, 2, 2)
    mixed = jnp.einsum('pqab,larb->lprq', gate_four, quad, precision=lax.Precision.HIGHEST)
    theta = mixed.reshape(ROWS, ROWS).astype(jnp.bfloat16)
    sketch = jnp.dot(theta.astype(jnp.float32), omega.astype(jnp.float32), preferred_element_type=jnp.float32)
    gram = jnp.dot(sketch.T, sketch, precision=lax.Precision.HIGHEST) / ROWS
    factor = jnp.linalg.cholesky(gram)
    basis = jax.scipy.linalg.solve_triangular(factor, sketch.T, lower=True).T
    projected = jnp.dot(basis.T, theta.astype(jnp.float32), precision=lax.Precision.HIGHEST) / math.sqrt(ROWS)
    return (basis, projected)
```

```python
import functools

import jax
import jax.numpy as jnp
import numpy as np
from jax import lax
from jax.experimental import pallas as pl
from jax.experimental.pallas import tpu as pltpu
from jax.sharding import Mesh
from jax.sharding import PartitionSpec as P

HI = lax.Precision.HIGHEST
F32, BF16 = jnp.float32, jnp.bfloat16
TILE = 256
HALF = 128
VMEM_LIMIT = 60 << 20
WHOLE = pl.BlockSpec(memory_space=pltpu.VMEM)


def split(x):
    head = x.astype(BF16)
    return head, (x - head.astype(F32)).astype(BF16)


def tdot(a, b, precision=None):
    return lax.dot_general(
        a, b, (((0,), (0,)), ((), ())), preferred_element_type=F32, precision=precision
    )


def front_kernel(gate_ref, left_ref, right_ref, omega_ref, theta_ref, sketch_ref, bond_ref):
    groups, lanes_x, part, rows = left_ref.shape
    for xs in range(lanes_x):
        for zc in range(groups):
            at = (xs * groups + zc) * part
            bond_ref[at : at + part, :] = left_ref[zc, xs]
    width = right_ref.shape[2]
    left = bond_ref[...]
    row_odd = lax.broadcasted_iota(jnp.int32, (rows, width), 0) % 2 == 1
    col_odd = lax.broadcasted_iota(jnp.int32, (rows, width), 1) % 2 == 1

    def coupling(row_flip, col_flip):
        def entry(s1, s2):
            a, b = s1 ^ row_flip, s2 ^ col_flip
            return gate_ref[2 * s1 + s2, 2 * a + b]

        even = jnp.where(col_odd, entry(0, 1), entry(0, 0))
        odd = jnp.where(col_odd, entry(1, 1), entry(1, 0))
        return jnp.where(row_odd, odd, even)

    for xs in range(right_ref.shape[0]):
        bare = tdot(left, right_ref[xs])
        row_partner = jnp.where(row_odd, pltpu.roll(bare, 1, 0), pltpu.roll(bare, rows - 1, 0))

        def col_partner(v):
            return jnp.where(col_odd, pltpu.roll(v, 1, 1), pltpu.roll(v, width - 1, 1))

        mixed = (coupling(0, 0) * bare + coupling(0, 1) * col_partner(bare)) + (
            coupling(1, 0) * row_partner + coupling(1, 1) * col_partner(row_partner)
        )
        theta_ref[:, xs * width : (xs + 1) * width] = mixed.astype(BF16)
    theta = theta_ref[...]
    step = omega_ref.shape[2]
    for y in range(omega_ref.shape[0]):
        sketch_ref[:, y * step : (y + 1) * step] = jnp.dot(
            theta, omega_ref[y], preferred_element_type=F32
        )


def front(gate, left, right, omega):
    rows = left.shape[3]
    bond = right.shape[1]
    cols = right.shape[0] * right.shape[2]
    k = omega.shape[0] * omega.shape[2]
    return pl.pallas_call(
        front_kernel,
        out_shape=(jax.ShapeDtypeStruct((rows, cols), BF16), jax.ShapeDtypeStruct((rows, k), F32)),
        in_specs=[pl.BlockSpec(memory_space=pltpu.SMEM), WHOLE, WHOLE, WHOLE],
        out_specs=(WHOLE, WHOLE),
        scratch_shapes=[pltpu.VMEM((bond, rows), BF16)],
        compiler_params=pltpu.CompilerParams(vmem_limit_bytes=VMEM_LIMIT),
        name="front",
    )(gate, left, right, omega)


def gram_kernel(scale, per, group_ref, i_ref, j_ref, s_ref, out_ref):
    chunks, piece = out_ref.shape[0], out_ref.shape[2]

    def tile(t, carry):
        at = group_ref[0] * per + t
        i = pl.multiple_of(i_ref[at] * TILE, TILE)
        j = pl.multiple_of(j_ref[at] * TILE, TILE)
        value = tdot(s_ref[:, pl.ds(i, TILE)], s_ref[:, pl.ds(j, TILE)], HI) * scale
        out_ref[:, pl.ds(t, 1)] = value.reshape(chunks, 1, piece, TILE)
        return carry

    lax.fori_loop(0, per, tile, 0)


def gram(sketch, group, pairs, per, chunks, scale):
    smem = pl.BlockSpec(memory_space=pltpu.SMEM)
    return pl.pallas_call(
        functools.partial(gram_kernel, scale, per),
        out_shape=jax.ShapeDtypeStruct((chunks, per, TILE // chunks, TILE), F32),
        in_specs=[smem, smem, smem, WHOLE],
        out_specs=WHOLE,
        compiler_params=pltpu.CompilerParams(vmem_limit_bytes=VMEM_LIMIT),
        name="gram",
    )(group, pairs[0], pairs[1], sketch)


def cross_kernel(scale, s_ref, theta_ref, out_ref):
    parts, _, width = out_ref.shape
    for at in range(0, s_ref.shape[1], TILE):
        head, rest = split(s_ref[:, at : at + TILE])
        value = (tdot(head, theta_ref[...]) + tdot(rest, theta_ref[...])) * scale
        for x in range(parts):
            out_ref[x, at : at + TILE, :] = value[:, x * width : (x + 1) * width]


def cross(sketch, theta, parts, scale):
    width = theta.shape[1] // parts
    return pl.pallas_call(
        functools.partial(cross_kernel, scale),
        out_shape=jax.ShapeDtypeStruct((parts, sketch.shape[1], width), F32),
        in_specs=[WHOLE, WHOLE],
        out_specs=WHOLE,
        compiler_params=pltpu.CompilerParams(vmem_limit_bytes=VMEM_LIMIT),
        name="cross",
    )(sketch, theta)


def leaf(rows):
    lane = lax.broadcasted_iota(jnp.int32, (8, HALF), 1)
    sub = lax.broadcasted_iota(jnp.int32, (8, HALF), 0)
    rows = list(rows)
    count = len(rows)
    done = []
    for j in range(count):
        base = 8 * j
        here = (lane >= base) & (lane < base + 8)
        part = rows[j]
        cols = [jnp.broadcast_to(part[:, base + k : base + k + 1], (8, HALF)) for k in range(8)]
        part = jnp.where(here, jnp.where(lane - base == sub, 1.0, 0.0), part)
        tri = jnp.zeros((8, HALF), F32)
        for k in range(8):
            at = sub == k
            pivot = jnp.broadcast_to(cols[k][k : k + 1, :], (8, HALF))
            inv = 1.0 / pivot
            row = jnp.broadcast_to(part[k : k + 1, :], (8, HALF))
            tri = jnp.where(at, row * lax.rsqrt(pivot), tri)
            factor = cols[k] * inv
            part = jnp.where(at, row * inv, part - factor * row)
            for m in range(k + 1, 8):
                mrow = jnp.broadcast_to(cols[m][k : k + 1, :], (8, HALF))
                cols[m] = jnp.where(at, mrow * inv, cols[m] - factor * mrow)
        done.append(jnp.where(lane < base + 8, tri, 0.0))
        if j + 1 < count:
            prow = [jnp.broadcast_to(part[k : k + 1, :], (8, HALF)) for k in range(8)]
            for i in range(j + 1, count):
                mine = rows[i]
                terms = [
                    jnp.broadcast_to(mine[:, base + k : base + k + 1], (8, HALF)) * prow[k]
                    for k in range(8)
                ]
                while len(terms) > 1:
                    terms = [terms[q] + terms[q + 1] for q in range(0, len(terms), 2)]
                rows[i] = jnp.where(here, 0.0, mine) - terms[0]
    return done


def factor_kernel(
    pairs, per, g_ref, uh_ref, ul_ref, inv_ref, grid_ref, a_ref, l1_ref, l2_ref, sem
):
    blocks, piece, n = grid_ref.shape
    t_ref = grid_ref.reshape(n, n)
    nt = n // TILE
    chunks = TILE // piece
    groups = g_ref.shape[0] // chunks
    source = g_ref.reshape(chunks, groups, per, piece, TILE)

    def fetch(at):
        i, j = pairs[at]
        return pltpu.make_async_copy(
            source.at[:, at // per, at % per],
            grid_ref.at[pl.ds(i * chunks, chunks), :, pl.ds(j * TILE, TILE)],
            sem.at[min(i, 1)],
        )

    for at in range(len(pairs)):
        fetch(at).start()
    for at in range(len(pairs)):
        if pairs[at][0] == 0:
            fetch(at).wait()

    def factor(l_ref):
        out = leaf([a_ref[8 * i : 8 * i + 8, :] for i in range(HALF // 8)])
        for i, rows in enumerate(out):
            l_ref[8 * i : 8 * i + 8, :] = rows

    def panel(p, carry):
        base = pl.multiple_of(p * TILE, TILE)
        mid = pl.multiple_of(p * TILE + HALF, HALF)
        a_ref[...] = t_ref[pl.ds(base, HALF), pl.ds(base, HALF)]
        factor(l1_ref)
        l1 = l1_ref[...]
        uab = jnp.dot(l1, t_ref[pl.ds(base, HALF), pl.ds(mid, HALF)], precision=HI)
        a_ref[...] = t_ref[pl.ds(mid, HALF), pl.ds(mid, HALF)] - tdot(uab, uab, HI)
        factor(l2_ref)
        l2 = l2_ref[...]
        l21 = -jnp.dot(l2, tdot(uab, l1, HI), precision=HI)
        inv_ref[p, 0:HALF, 0:HALF] = l1
        inv_ref[p, 0:HALF, HALF:] = jnp.zeros((HALF, HALF), F32)
        inv_ref[p, HALF:, 0:HALF] = l21
        inv_ref[p, HALF:, HALF:] = l2

        @pl.when(p == 0)
        def _():
            for at in range(len(pairs)):
                if pairs[at][0] != 0:
                    fetch(at).wait()

        def row_tile(c, carry):
            at = pl.multiple_of(c * TILE, TILE)
            u = jnp.dot(inv_ref[p], t_ref[pl.ds(base, TILE), pl.ds(at, TILE)], precision=HI)
            head, rest = split(u)
            uh_ref[pl.ds(base, TILE), pl.ds(at, TILE)] = head
            ul_ref[pl.ds(base, TILE), pl.ds(at, TILE)] = rest
            return carry

        lax.fori_loop(p + 1, nt, row_tile, 0)

        def trail_row(r, carry):
            rat = pl.multiple_of(r * TILE, TILE)
            head = uh_ref[pl.ds(base, TILE), pl.ds(rat, TILE)].T
            rest = ul_ref[pl.ds(base, TILE), pl.ds(rat, TILE)].T

            def trail(c, carry):
                cat = pl.multiple_of(c * TILE, TILE)
                ch = uh_ref[pl.ds(base, TILE), pl.ds(cat, TILE)]
                cl = ul_ref[pl.ds(base, TILE), pl.ds(cat, TILE)]
                update = jnp.dot(head, ch, preferred_element_type=F32) + (
                    jnp.dot(head, cl, preferred_element_type=F32)
                    + jnp.dot(rest, ch, preferred_element_type=F32)
                )
                t_ref[pl.ds(rat, TILE), pl.ds(cat, TILE)] -= update
                return carry

            lax.fori_loop(r, nt, trail, 0)
            return carry

        lax.fori_loop(p + 1, nt, trail_row, 0)
        return carry

    lax.fori_loop(0, nt, panel, 0)


def factorize(tiles, n, pairs, per):
    piece = tiles.shape[2]
    return pl.pallas_call(
        functools.partial(factor_kernel, pairs, per),
        out_shape=(
            jax.ShapeDtypeStruct((n, n), BF16),
            jax.ShapeDtypeStruct((n, n), BF16),
            jax.ShapeDtypeStruct((n // TILE, TILE, TILE), F32),
        ),
        in_specs=[pl.BlockSpec(memory_space=pl.ANY)],
        out_specs=(WHOLE,) * 3,
        scratch_shapes=[
            pltpu.VMEM((n // piece, piece, n), F32),
            pltpu.VMEM((HALF, HALF), F32),
            pltpu.VMEM((HALF, HALF), F32),
            pltpu.VMEM((HALF, HALF), F32),
            pltpu.SemaphoreType.DMA((2,)),
        ],
        compiler_params=pltpu.CompilerParams(vmem_limit_bytes=VMEM_LIMIT),
        cost_estimate=pl.CostEstimate(
            flops=2 * n**3, bytes_accessed=n * n * 8, transcendentals=0
        ),
        name="factorize",
    )(tiles)


def solve_kernel(nt, uh_ref, ul_ref, inv_ref, s_ref, w_ref, basis_ref, proj_ref, y_ref):
    p = pl.program_id(0)
    mine, n = s_ref.shape

    @pl.when(p == 0)
    def _():
        padded = jnp.concatenate([s_ref[...], jnp.zeros((HALF - mine, n), F32)], axis=0)
        y_ref[:, :HALF] = padded.T
        y_ref[:, HALF:] = w_ref[...]

    base = pl.multiple_of(p * TILE, TILE)
    y = jnp.dot(inv_ref[0], y_ref[pl.ds(base, TILE), :], precision=HI)
    y_ref[pl.ds(base, TILE), :] = y
    proj_ref[pl.ds(base, TILE), :] = y[:, HALF:]
    head, rest = split(y)

    def tail(r, carry):
        at = pl.multiple_of(r * TILE, TILE)
        uh = uh_ref[:, pl.ds(at, TILE)]
        ul = ul_ref[:, pl.ds(at, TILE)]
        y_ref[pl.ds(at, TILE), :] -= tdot(uh, head) + (tdot(uh, rest) + tdot(ul, head))
        return carry

    lax.fori_loop(p + 1, nt, tail, 0)

    @pl.when(p == nt - 1)
    def _():
        basis_ref[...] = y_ref[:, :HALF].T[:mine]


def solve(uh, ul, inv, sketch, weights):
    mine, n = sketch.shape
    nt = n // TILE
    fixed = lambda p: (0, 0)
    return pl.pallas_call(
        functools.partial(solve_kernel, nt),
        grid=(nt,),
        out_shape=(jax.ShapeDtypeStruct((mine, n), F32), jax.ShapeDtypeStruct((n, HALF), F32)),
        in_specs=[
            pl.BlockSpec((TILE, n), lambda p: (p, 0)),
            pl.BlockSpec((TILE, n), lambda p: (p, 0)),
            pl.BlockSpec((1, TILE, TILE), lambda p: (p, 0, 0)),
            pl.BlockSpec((mine, n), fixed),
            pl.BlockSpec((n, HALF), fixed),
        ],
        out_specs=(pl.BlockSpec((mine, n), fixed), pl.BlockSpec((n, HALF), fixed)),
        scratch_shapes=[pltpu.VMEM((n, 2 * HALF), F32)],
        compiler_params=pltpu.CompilerParams(vmem_limit_bytes=VMEM_LIMIT),
        name="solve",
    )(uh, ul, inv, sketch, weights)


def tile_pairs(nt, groups):
    pairs = [(i, j) for i in range(nt) for j in range(i, nt)]
    per = -(-len(pairs) // groups)
    return pairs, per


def on_device(left_site, right_site, gate, omega):
    ny, nx, nz, nc = (lax.axis_size(a) for a in ("row", "x", "z", "core"))
    groups = nz * nc
    rows_y, part = left_site.shape
    rows = rows_y // nx
    total = rows_y * ny
    zc = lax.axis_index("z") * nc + lax.axis_index("core")

    left = left_site.T.reshape(part, nx, rows).transpose(1, 0, 2)
    left = lax.all_to_all(left, "x", 0, 0)
    left = lax.all_gather(left, ("z", "core"), axis=0)
    right = lax.all_gather(right_site, "row", axis=0, tiled=True)
    right = lax.all_gather(right, "x", axis=0)
    width = right_site.shape[1]
    omega_mine = lax.dynamic_slice_in_dim(
        omega.reshape(nx, groups, width, omega.shape[1]), zc, 1, 1
    ).reshape(nx * width, omega.shape[1])
    omega_all = lax.all_gather(omega_mine, "row", axis=0)

    theta, partial = front(gate, left, right, omega_all)
    sketch = lax.psum_scatter(partial, ("z", "core"), scatter_dimension=0, tiled=True)
    n = sketch.shape[1]
    sketch_rows = lax.all_gather(sketch, ("z", "core"), axis=0, tiled=True)

    pairs, per = tile_pairs(n // TILE, groups)
    padded = pairs + [(0, 0)] * (per * groups - len(pairs))
    table = jnp.asarray(np.array(padded, np.int32).T)
    mine = gram(sketch_rows, zc.reshape(1).astype(jnp.int32), table, per, ny * nx, 1.0 / total)
    mine = lax.psum_scatter(mine, ("row", "x"), scatter_dimension=0, tiled=True)
    tiles = lax.all_gather(mine, ("row", "x", "z", "core"), axis=0, tiled=True)

    weights = cross(sketch_rows, theta, nx, 1.0 / math_sqrt(total))
    tiles, weights = lax.optimization_barrier((tiles, weights))
    weights = lax.psum_scatter(weights, "x", scatter_dimension=0, tiled=True)
    weights = lax.psum(weights, "row").reshape(n, width)

    uh, ul, inv = factorize(tiles, n, pairs, per)
    basis, projected = solve(uh, ul, inv, sketch, weights)
    block = n // ny
    return basis, lax.dynamic_slice_in_dim(projected, lax.axis_index("row") * block, block, 0)


def math_sqrt(value):
    return float(np.sqrt(value))


def solution(mesh):
    fine = Mesh(mesh.devices.reshape(4, 4, 4, 2), ("row", "x", "z", "core"))
    col = ("x", "z", "core")
    in_specs = (P("row", col), P("row", col), P(), P(None, "row"))
    out_specs = (P(("row",) + col, None), P("row", col))
    return jax.shard_map(on_device, mesh=fine, in_specs=in_specs, out_specs=out_specs, check_vma=False)
```

```python
import functools

import jax
import jax.numpy as jnp
import numpy as np
from jax import lax
from jax.experimental import pallas as pl
from jax.experimental.pallas import tpu as pltpu
from jax.sharding import Mesh
from jax.sharding import PartitionSpec as P

HI = lax.Precision.HIGHEST
F32, BF16 = jnp.float32, jnp.bfloat16
TILE = 256
HALF = 128
VMEM_LIMIT = 60 << 20
WHOLE = pl.BlockSpec(memory_space=pltpu.VMEM)


def split(x):
    head = x.astype(BF16)
    return head, (x - head.astype(F32)).astype(BF16)


def tdot(a, b, precision=None):
    return lax.dot_general(
        a, b, (((0,), (0,)), ((), ())), preferred_element_type=F32, precision=precision
    )


def front_kernel(gate_ref, left_ref, right_ref, omega_ref, theta_ref, sketch_ref, bond_ref):
    groups, lanes_x, part, rows = left_ref.shape
    for xs in range(lanes_x):
        for zc in range(groups):
            at = (xs * groups + zc) * part
            bond_ref[at : at + part, :] = left_ref[zc, xs]
    width = right_ref.shape[2]
    left = bond_ref[...]
    row_odd = lax.broadcasted_iota(jnp.int32, (rows, width), 0) % 2 == 1
    col_odd = lax.broadcasted_iota(jnp.int32, (rows, width), 1) % 2 == 1

    def coupling(row_flip, col_flip):
        def entry(s1, s2):
            a, b = s1 ^ row_flip, s2 ^ col_flip
            return gate_ref[2 * s1 + s2, 2 * a + b]

        even = jnp.where(col_odd, entry(0, 1), entry(0, 0))
        odd = jnp.where(col_odd, entry(1, 1), entry(1, 0))
        return jnp.where(row_odd, odd, even)

    for xs in range(right_ref.shape[0]):
        bare = tdot(left, right_ref[xs])
        row_partner = jnp.where(row_odd, pltpu.roll(bare, 1, 0), pltpu.roll(bare, rows - 1, 0))

        def col_partner(v):
            return jnp.where(col_odd, pltpu.roll(v, 1, 1), pltpu.roll(v, width - 1, 1))

        mixed = (coupling(0, 0) * bare + coupling(0, 1) * col_partner(bare)) + (
            coupling(1, 0) * row_partner + coupling(1, 1) * col_partner(row_partner)
        )
        theta_ref[:, xs * width : (xs + 1) * width] = mixed.astype(BF16)
    theta = theta_ref[...]
    step = omega_ref.shape[2]
    for y in range(omega_ref.shape[0]):
        sketch_ref[:, y * step : (y + 1) * step] = jnp.dot(
            theta, omega_ref[y], preferred_element_type=F32
        )


def front(gate, left, right, omega):
    rows = left.shape[3]
    bond = right.shape[1]
    cols = right.shape[0] * right.shape[2]
    k = omega.shape[0] * omega.shape[2]
    return pl.pallas_call(
        front_kernel,
        out_shape=(jax.ShapeDtypeStruct((rows, cols), BF16), jax.ShapeDtypeStruct((rows, k), F32)),
        in_specs=[pl.BlockSpec(memory_space=pltpu.SMEM), WHOLE, WHOLE, WHOLE],
        out_specs=(WHOLE, WHOLE),
        scratch_shapes=[pltpu.VMEM((bond, rows), BF16)],
        compiler_params=pltpu.CompilerParams(vmem_limit_bytes=VMEM_LIMIT),
        name="front",
    )(gate, left, right, omega)


def gram_kernel(scale, per, group_ref, i_ref, j_ref, s_ref, out_ref):
    chunks, piece = out_ref.shape[0], out_ref.shape[2]

    def tile(t, carry):
        at = group_ref[0] * per + t
        i = pl.multiple_of(i_ref[at] * TILE, TILE)
        j = pl.multiple_of(j_ref[at] * TILE, TILE)
        value = tdot(s_ref[:, pl.ds(i, TILE)], s_ref[:, pl.ds(j, TILE)], HI) * scale
        out_ref[:, pl.ds(t, 1)] = value.reshape(chunks, 1, piece, TILE)
        return carry

    lax.fori_loop(0, per, tile, 0)


def gram(sketch, group, pairs, per, chunks, scale):
    smem = pl.BlockSpec(memory_space=pltpu.SMEM)
    return pl.pallas_call(
        functools.partial(gram_kernel, scale, per),
        out_shape=jax.ShapeDtypeStruct((chunks, per, TILE // chunks, TILE), F32),
        in_specs=[smem, smem, smem, WHOLE],
        out_specs=WHOLE,
        compiler_params=pltpu.CompilerParams(vmem_limit_bytes=VMEM_LIMIT),
        name="gram",
    )(group, pairs[0], pairs[1], sketch)


def cross_kernel(scale, s_ref, theta_ref, out_ref):
    parts, _, width = out_ref.shape
    for at in range(0, s_ref.shape[1], TILE):
        head, rest = split(s_ref[:, at : at + TILE])
        value = (tdot(head, theta_ref[...]) + tdot(rest, theta_ref[...])) * scale
        for x in range(parts):
            out_ref[x, at : at + TILE, :] = value[:, x * width : (x + 1) * width]


def cross(sketch, theta, parts, scale):
    width = theta.shape[1] // parts
    return pl.pallas_call(
        functools.partial(cross_kernel, scale),
        out_shape=jax.ShapeDtypeStruct((parts, sketch.shape[1], width), F32),
        in_specs=[WHOLE, WHOLE],
        out_specs=WHOLE,
        compiler_params=pltpu.CompilerParams(vmem_limit_bytes=VMEM_LIMIT),
        name="cross",
    )(sketch, theta)


def leaf(rows):
    lane = lax.broadcasted_iota(jnp.int32, (8, HALF), 1)
    sub = lax.broadcasted_iota(jnp.int32, (8, HALF), 0)
    rows = list(rows)
    count = len(rows)
    done = []
    for j in range(count):
        base = 8 * j
        here = (lane >= base) & (lane < base + 8)
        part = rows[j]
        cols = [jnp.broadcast_to(part[:, base + k : base + k + 1], (8, HALF)) for k in range(8)]
        part = jnp.where(here, jnp.where(lane - base == sub, 1.0, 0.0), part)
        tri = jnp.zeros((8, HALF), F32)
        for k in range(8):
            at = sub == k
            pivot = jnp.broadcast_to(cols[k][k : k + 1, :], (8, HALF))
            inv = 1.0 / pivot
            row = jnp.broadcast_to(part[k : k + 1, :], (8, HALF))
            tri = jnp.where(at, row * lax.rsqrt(pivot), tri)
            factor = cols[k] * inv
            part = jnp.where(at, row * inv, part - factor * row)
            for m in range(k + 1, 8):
                mrow = jnp.broadcast_to(cols[m][k : k + 1, :], (8, HALF))
                cols[m] = jnp.where(at, mrow * inv, cols[m] - factor * mrow)
        done.append(jnp.where(lane < base + 8, tri, 0.0))
        if j + 1 < count:
            prow = [jnp.broadcast_to(part[k : k + 1, :], (8, HALF)) for k in range(8)]
            for i in range(j + 1, count):
                mine = rows[i]
                terms = [
                    jnp.broadcast_to(mine[:, base + k : base + k + 1], (8, HALF)) * prow[k]
                    for k in range(8)
                ]
                while len(terms) > 1:
                    terms = [terms[q] + terms[q + 1] for q in range(0, len(terms), 2)]
                rows[i] = jnp.where(here, 0.0, mine) - terms[0]
    return done


def stage_kernel(plan, per, *refs):
    first, stop, nt, chunks, has_carry, has_tiles = plan
    refs = list(refs)
    g_ref = refs.pop(0) if has_tiles else None
    carry_ref = refs.pop(0) if has_carry else None
    uh_ref, ul_ref, inv_ref = refs[:3]
    refs = refs[3:]
    last = stop == nt
    out_ref = None if last else refs.pop(0)
    grid_ref, a_ref, l_ref, uab_ref, sem = refs[:5]
    extra_ref = refs[5] if has_carry and has_tiles else None
    m = (nt - first) * TILE
    size = nt - first
    count = stop - first
    t_ref = grid_ref.reshape(m, m)
    copies = []
    if has_tiles:
        groups = g_ref.shape[0] // chunks
        source = g_ref.reshape(chunks, groups, per, TILE // chunks, TILE)
        target = grid_ref if extra_ref is None else extra_ref
        low, high = (first, stop) if not has_carry else (first, nt)
        for at, (i, j) in enumerate((i, j) for i in range(low, high) for j in range(i, nt)):
            rows = pl.ds((i - first) * chunks, chunks)
            cols = pl.ds((j - first) * TILE, TILE)
            copies.append(
                pltpu.make_async_copy(
                    source.at[:, at // per, at % per], target.at[rows, :, cols], sem.at[0]
                )
            )
    if has_carry:
        for i in range(size):
            at = pl.ds(i * TILE, TILE)
            cols = pl.ds(i * TILE, m - i * TILE)
            copies.append(pltpu.make_async_copy(carry_ref.at[at, cols], t_ref.at[at, cols], sem.at[1]))
    for copy in copies:
        copy.start()
    if not has_carry and not last:
        t_ref[count * TILE :, count * TILE :] = jnp.zeros((m - count * TILE,) * 2, F32)
    for copy in copies:
        copy.wait()
    if extra_ref is not None:
        e_ref = extra_ref.reshape(m, m)

        def add_row(r, carry):
            rat = pl.multiple_of(r * TILE, TILE)

            def add(c, carry):
                cat = pl.multiple_of(c * TILE, TILE)
                t_ref[pl.ds(rat, TILE), pl.ds(cat, TILE)] += e_ref[pl.ds(rat, TILE), pl.ds(cat, TILE)]
                return carry

            return lax.fori_loop(r, size, add, carry)

        lax.fori_loop(0, size, add_row, 0)

    def half(p, h, carry):
        base = pl.multiple_of(p * TILE, TILE)
        mid = pl.multiple_of(p * TILE + HALF, HALF)

        @pl.when(h == 0)
        def _():
            a_ref[...] = t_ref[pl.ds(base, HALF), pl.ds(base, HALF)]

        @pl.when(h == 1)
        def _():
            a_ref[...] = t_ref[pl.ds(mid, HALF), pl.ds(mid, HALF)] - tdot(uab_ref[...], uab_ref[...], HI)

        out = leaf([a_ref[8 * i : 8 * i + 8, :] for i in range(HALF // 8)])
        for i, rows in enumerate(out):
            l_ref[8 * i : 8 * i + 8, :] = rows

        @pl.when(h == 0)
        def _():
            inv_ref[p, 0:HALF, 0:HALF] = l_ref[...]
            inv_ref[p, 0:HALF, HALF:] = jnp.zeros((HALF, HALF), F32)
            uab_ref[...] = jnp.dot(
                l_ref[...], t_ref[pl.ds(base, HALF), pl.ds(mid, HALF)], precision=HI
            )

        @pl.when(h == 1)
        def _():
            cross = tdot(uab_ref[...], inv_ref[p, 0:HALF, 0:HALF], HI)
            inv_ref[p, HALF:, 0:HALF] = -jnp.dot(l_ref[...], cross, precision=HI)
            inv_ref[p, HALF:, HALF:] = l_ref[...]

        return carry

    def panel(p, carry):
        base = pl.multiple_of(p * TILE, TILE)
        lax.fori_loop(0, 2, functools.partial(half, p), 0)

        def row_tile(c, carry):
            at = pl.multiple_of(c * TILE, TILE)
            u = jnp.dot(inv_ref[p], t_ref[pl.ds(base, TILE), pl.ds(at, TILE)], precision=HI)
            head, rest = split(u)
            uh_ref[pl.ds(base, TILE), pl.ds(at, TILE)] = head
            ul_ref[pl.ds(base, TILE), pl.ds(at, TILE)] = rest
            return carry

        lax.fori_loop(p + 1, size, row_tile, 0)

        def trail_row(r, carry):
            rat = pl.multiple_of(r * TILE, TILE)
            head = uh_ref[pl.ds(base, TILE), pl.ds(rat, TILE)].T
            rest = ul_ref[pl.ds(base, TILE), pl.ds(rat, TILE)].T

            def trail(c, carry):
                cat = pl.multiple_of(c * TILE, TILE)
                ch = uh_ref[pl.ds(base, TILE), pl.ds(cat, TILE)]
                cl = ul_ref[pl.ds(base, TILE), pl.ds(cat, TILE)]
                update = jnp.dot(head, ch, preferred_element_type=F32) + (
                    jnp.dot(head, cl, preferred_element_type=F32)
                    + jnp.dot(rest, ch, preferred_element_type=F32)
                )
                t_ref[pl.ds(rat, TILE), pl.ds(cat, TILE)] -= update
                return carry

            lax.fori_loop(r, size, trail, 0)
            return carry

        lax.fori_loop(p + 1, size, trail_row, 0)
        return carry

    lax.fori_loop(0, count, panel, 0)
    if out_ref is not None:
        back = []
        for i in range(count, size):
            at = pl.ds((i - count) * TILE, TILE)
            cols = pl.ds((i - count) * TILE, m - i * TILE)
            mine = t_ref.at[pl.ds(i * TILE, TILE), pl.ds(i * TILE, m - i * TILE)]
            back.append(pltpu.make_async_copy(mine, out_ref.at[at, cols], sem.at[0]))
        for copy in back:
            copy.start()
        for copy in back:
            copy.wait()


def stage(first, stop, n, per, chunks, tiles=None, carry=None):
    nt = n // TILE
    m = n - first * TILE
    rows = (stop - first) * TILE
    piece = TILE // chunks
    args = [v for v in (tiles, carry) if v is not None]
    out_shape = [
        jax.ShapeDtypeStruct((rows, m), BF16),
        jax.ShapeDtypeStruct((rows, m), BF16),
        jax.ShapeDtypeStruct((stop - first, TILE, TILE), F32),
    ]
    out_specs = [WHOLE] * 3
    if stop < nt:
        out_shape.append(jax.ShapeDtypeStruct((m - rows, m - rows), F32))
        out_specs.append(pl.BlockSpec(memory_space=pl.ANY))
    scratch = [
        pltpu.VMEM((m // piece, piece, m), F32),
        pltpu.VMEM((HALF, HALF), F32),
        pltpu.VMEM((HALF, HALF), F32),
        pltpu.VMEM((HALF, HALF), F32),
        pltpu.SemaphoreType.DMA((2,)),
    ]
    if len(args) == 2:
        scratch.append(pltpu.VMEM((m // piece, piece, m), F32))
    plan = (first, stop, nt, chunks, carry is not None, tiles is not None)
    return pl.pallas_call(
        functools.partial(stage_kernel, plan, per),
        out_shape=tuple(out_shape),
        in_specs=[pl.BlockSpec(memory_space=pl.ANY)] * len(args),
        out_specs=tuple(out_specs),
        scratch_shapes=scratch,
        compiler_params=pltpu.CompilerParams(vmem_limit_bytes=VMEM_LIMIT),
        cost_estimate=pl.CostEstimate(
            flops=40 * 10**9, bytes_accessed=rows * m * 8, transcendentals=0
        ),
        name=f"stage{first}",
    )(*args)


def solve_kernel(plan, *refs):
    stages = len(plan)
    factors = refs[: 3 * stages]
    s_ref, w_ref, basis_ref, proj_ref, y_ref = refs[3 * stages : 3 * stages + 5]
    held = refs[3 * stages + 5 : 6 * stages + 5]
    sem = refs[6 * stages + 5]
    copies = [
        pltpu.make_async_copy(a, b, sem.at[q]) for q, (a, b) in enumerate(zip(factors, held))
    ]
    for copy in copies:
        copy.start()
    mine, n = s_ref.shape
    nt = n // TILE
    padded = jnp.concatenate([s_ref[...], jnp.zeros((HALF - mine, n), F32)], axis=0)
    y_ref[:, :HALF] = padded.T
    y_ref[:, HALF:] = w_ref[...]
    for q, (first, stop) in enumerate(plan):
        uh_ref, ul_ref, inv_ref = held[3 * q : 3 * q + 3]
        for copy in copies[3 * q : 3 * q + 3]:
            copy.wait()
        for p in range(first, stop):
            rows = slice(p * TILE, (p + 1) * TILE)
            local = slice((p - first) * TILE, (p - first + 1) * TILE)
            y = jnp.dot(inv_ref[p - first], y_ref[rows, :], precision=HI)
            y_ref[rows, :] = y
            proj_ref[rows, :] = y[:, HALF:]
            head, rest = split(y)

            def tail(r, carry):
                at = pl.multiple_of(r * TILE, TILE)
                here = pl.multiple_of((r - first) * TILE, TILE)
                uh = uh_ref[local, pl.ds(here, TILE)]
                ul = ul_ref[local, pl.ds(here, TILE)]
                y_ref[pl.ds(at, TILE), :] -= tdot(uh, head) + (tdot(uh, rest) + tdot(ul, head))
                return carry

            lax.fori_loop(p + 1, nt, tail, 0)
    basis_ref[...] = y_ref[:, :HALF].T[:mine]


def solve(plan, factors, sketch, weights):
    mine, n = sketch.shape
    flat = [v for part in factors for v in part]
    return pl.pallas_call(
        functools.partial(solve_kernel, plan),
        out_shape=(jax.ShapeDtypeStruct((mine, n), F32), jax.ShapeDtypeStruct((n, HALF), F32)),
        in_specs=[pl.BlockSpec(memory_space=pl.ANY)] * len(flat) + [WHOLE, WHOLE],
        out_specs=(WHOLE, WHOLE),
        scratch_shapes=[pltpu.VMEM((n, 2 * HALF), F32)]
        + [pltpu.VMEM(v.shape, v.dtype) for v in flat]
        + [pltpu.SemaphoreType.DMA((len(flat),))],
        compiler_params=pltpu.CompilerParams(vmem_limit_bytes=VMEM_LIMIT),
        name="solve",
    )(*flat, sketch, weights)


CUTS = ((0, 3), (3, 6), (6, 9))


def tile_table(nt, groups):
    cut = CUTS[0][1]
    parts = [
        [(i, j) for i in range(low, high) for j in range(i, nt)] for low, high in ((0, cut), (cut, nt))
    ]
    per = -(-max(len(part) for part in parts) // groups)
    padded = [part + [(0, 0)] * (per * groups - len(part)) for part in parts]
    dealt = [
        padded[half][g * per + t] for g in range(groups) for half in range(2) for t in range(per)
    ]
    return np.array(dealt, np.int32).T, per


def on_device(left_site, right_site, gate, omega):
    ny, nx, nz, nc = (lax.axis_size(a) for a in ("row", "x", "z", "core"))
    groups = nz * nc
    rows_y, part = left_site.shape
    rows = rows_y // nx
    total = rows_y * ny
    zc = lax.axis_index("z") * nc + lax.axis_index("core")

    left = left_site.T.reshape(part, nx, rows).transpose(1, 0, 2)
    left = lax.all_to_all(left, "x", 0, 0)
    left = lax.all_gather(left, ("z", "core"), axis=0)
    right = lax.all_gather(right_site, "row", axis=0, tiled=True)
    right = lax.all_gather(right, "x", axis=0)
    width = right_site.shape[1]
    omega_mine = lax.dynamic_slice_in_dim(
        omega.reshape(nx, groups, width, omega.shape[1]), zc, 1, 1
    ).reshape(nx * width, omega.shape[1])
    omega_all = lax.all_gather(omega_mine, "row", axis=0)

    theta, partial = front(gate, left, right, omega_all)
    sketch = lax.psum_scatter(partial, ("z", "core"), scatter_dimension=0, tiled=True)
    n = sketch.shape[1]
    sketch_rows = lax.all_gather(sketch, ("z", "core"), axis=0, tiled=True)

    table, per = tile_table(n // TILE, groups)
    group = zc.reshape(1).astype(jnp.int32)
    chunks = ny * nx
    mine = gram(sketch_rows, group, jnp.asarray(table), 2 * per, chunks, 1.0 / total)
    mine = lax.psum_scatter(mine, "row", scatter_dimension=0, tiled=True)
    mine = lax.psum_scatter(mine, "x", scatter_dimension=0, tiled=True)
    everywhere = ("row", "x", "z", "core")
    early = lax.all_gather(mine[:, :per], everywhere, axis=0, tiled=True)
    weights = cross(sketch_rows, theta, nx, 1.0 / math_sqrt(total))
    early, late, weights = lax.optimization_barrier((early, mine[:, per:], weights))
    late = lax.all_gather(late, everywhere, axis=0, tiled=True)
    weights = lax.psum_scatter(weights, "x", scatter_dimension=0, tiled=True)

    *part_a, carry = stage(*CUTS[0], n, per, chunks, tiles=early)
    *part_b, carry = stage(*CUTS[1], n, per, chunks, tiles=late, carry=carry)
    carry, weights = lax.optimization_barrier((carry, weights))
    weights = lax.psum(weights, "row").reshape(n, width)
    part_c = stage(*CUTS[2], n, per, chunks, carry=carry)
    basis, projected = solve(CUTS, (part_a, part_b, part_c), sketch, weights)
    block = n // ny
    return basis, lax.dynamic_slice_in_dim(projected, lax.axis_index("row") * block, block, 0)


def math_sqrt(value):
    return float(np.sqrt(value))


def solution(mesh):
    fine = Mesh(mesh.devices.reshape(4, 4, 4, 2), ("row", "x", "z", "core"))
    col = ("x", "z", "core")
    in_specs = (P("row", col), P("row", col), P(), P(None, "row"))
    out_specs = (P(("row",) + col, None), P("row", col))
    return jax.shard_map(on_device, mesh=fine, in_specs=in_specs, out_specs=out_specs, check_vma=False)
```

```python
import functools

import jax
import jax.numpy as jnp
import numpy as np
from jax import lax
from jax.experimental import pallas as pl
from jax.experimental.pallas import tpu as pltpu
from jax.sharding import Mesh
from jax.sharding import PartitionSpec as P

HI = lax.Precision.HIGHEST
F32, BF16 = jnp.float32, jnp.bfloat16
TILE = 256
HALF = 128
VMEM_LIMIT = 60 << 20
WHOLE = pl.BlockSpec(memory_space=pltpu.VMEM)


def split(x):
    head = x.astype(BF16)
    return head, (x - head.astype(F32)).astype(BF16)


def tdot(a, b, precision=None):
    return lax.dot_general(
        a, b, (((0,), (0,)), ((), ())), preferred_element_type=F32, precision=precision
    )


def around(index, size, step):
    return lax.rem(index + step, size)


def front_kernel(
    sizes, per, scale, gate_ref, left_ref, right_ref, omega_hbm,
    theta_ref, rows_ref, mine_ref, tiles_ref,
    mine_left, all_left, all_right, all_omega, bond_ref,
    part_ref, pair_ref, sent_ref, got_ref, held_ref, gram_ref, grams_ref,
    local, o_send, o_recv, r_send, r_recv, l_send, l_recv, g_send, g_recv, pair_send, pair_recv, z_send, z_recv, b_send, b_recv, f_send, f_recv,
):
    ny, nx, nz, nc = sizes
    groups = nz * nc
    y, x, z, c = (lax.axis_index(a) for a in ("row", "x", "z", "core"))
    zc = z * nc + c
    other = 1 - c
    mesh = pl.DeviceIdType.MESH
    part, rows = mine_left.shape[1:]
    bond_y, width = right_ref.shape
    step = omega_hbm.shape[1]

    def push(src, dst, s, r, to):
        return pltpu.make_async_remote_copy(
            src_ref=src, dst_ref=dst, send_sem=s, recv_sem=r, device_id=to, device_id_type=mesh
        )

    for q in range(nx):
        mine_left[q] = left_ref[q * rows : (q + 1) * rows, :].T
    omega_moves, own_moves, right_moves, left_moves = [], [], [], []
    source = omega_hbm.reshape(nx, groups * width, step)
    src = source.at[:, pl.ds(pl.multiple_of(zc * width, width), width), :]
    own_moves.append(pltpu.make_async_copy(src, all_omega.at[y], local))
    for dy in range(1, ny):
        to = (around(y, ny, dy), x, z, c)
        omega_moves.append(push(src, all_omega.at[y], o_send.at[dy - 1], o_recv.at[dy - 1], to))
    home = all_right.at[x, pl.ds(pl.multiple_of(y * bond_y, bond_y), bond_y), :]
    for dy in range(ny):
        for dx in range(nx):
            if dy or dx:
                to = (around(y, ny, dy), around(x, nx, dx), z, c)
                at = len(right_moves)
                right_moves.append(push(right_ref, home, r_send.at[at], r_recv.at[at], to))
    for dx in range(nx):
        to_x = around(x, nx, dx)
        for dz in range(nz):
            for dc in range(nc):
                if dx or dz or dc:
                    to = (y, to_x, around(z, nz, dz), around(c, nc, dc))
                    at = len(left_moves)
                    left_moves.append(
                        push(mine_left.at[to_x], all_left.at[zc, x], l_send.at[at], l_recv.at[at], to)
                    )
    for move in right_moves + left_moves + omega_moves + own_moves:
        move.start()
    all_left[zc, x] = mine_left[x]
    all_right[x, pl.ds(pl.multiple_of(y * bond_y, bond_y), bond_y), :] = right_ref[...]
    for move in right_moves + left_moves:
        move.wait_recv()

    for xs in range(nx):
        for g in range(groups):
            at = (xs * groups + g) * part
            bond_ref[at : at + part, :] = all_left[g, xs]
    left = bond_ref[...]
    row_odd = lax.broadcasted_iota(jnp.int32, (rows, width), 0) % 2 == 1
    col_odd = lax.broadcasted_iota(jnp.int32, (rows, width), 1) % 2 == 1

    def coupling(row_flip, col_flip):
        def entry(s1, s2):
            a, b = s1 ^ row_flip, s2 ^ col_flip
            return gate_ref[2 * s1 + s2, 2 * a + b]

        even = jnp.where(col_odd, entry(0, 1), entry(0, 0))
        odd = jnp.where(col_odd, entry(1, 1), entry(1, 0))
        return jnp.where(row_odd, odd, even)

    for xs in range(nx):
        bare = tdot(left, all_right[xs])
        row_partner = jnp.where(row_odd, pltpu.roll(bare, 1, 0), pltpu.roll(bare, rows - 1, 0))

        def col_partner(v):
            return jnp.where(col_odd, pltpu.roll(v, 1, 1), pltpu.roll(v, width - 1, 1))

        mixed = (coupling(0, 0) * bare + coupling(0, 1) * col_partner(bare)) + (
            coupling(1, 0) * row_partner + coupling(1, 1) * col_partner(row_partner)
        )
        theta_ref[:, xs * width : (xs + 1) * width] = mixed.astype(BF16)
    for move in own_moves:
        move.wait()
    for move in omega_moves:
        move.wait_recv()
    theta = theta_ref[...]
    band = rows // groups
    for q in range(ny):
        value = jnp.dot(theta, all_omega[q].reshape(nx * width, step), preferred_element_type=F32)
        part_ref[:, :, q * step : (q + 1) * step] = value.reshape(groups, band, step)

    pair_moves = []
    for dz in range(1, nz + 1):
        to_z = around(z, nz, dz)
        pair_moves.append(
            push(part_ref.at[to_z * nc + other], pair_ref.at[dz - 1], pair_send.at[dz - 1],
                 pair_recv.at[dz - 1], (y, x, z, other))
        )
    for move in pair_moves:
        move.start()
    z_moves = []
    for dz in range(1, nz):
        to_z = around(z, nz, dz)
        pair_moves[dz - 1].wait_recv()
        sent_ref[dz - 1] = part_ref[to_z * nc + c] + pair_ref[dz - 1]
        move = push(sent_ref.at[dz - 1], got_ref.at[dz - 1], z_send.at[dz - 1], z_recv.at[dz - 1],
                    (y, x, to_z, c))
        move.start()
        z_moves.append(move)
    pair_moves[nz - 1].wait_recv()
    total = part_ref[zc] + pair_ref[nz - 1]
    for dz in range(1, nz):
        z_moves[dz - 1].wait_recv()
        total = total + got_ref[dz - 1]
    held_ref[zc] = total
    mine_ref[...] = total

    b_moves, f_moves = [], []
    for dz in range(1, nz):
        b_moves.append(
            push(held_ref.at[zc], held_ref.at[zc], b_send.at[dz - 1], b_recv.at[dz - 1],
                 (y, x, around(z, nz, dz), c))
        )
    for dz in range(nz):
        slot = around(z, nz, nz - dz) * nc + c
        f_moves.append(
            push(held_ref.at[slot], held_ref.at[slot], f_send.at[dz], f_recv.at[dz], (y, x, z, other))
        )
    for move in b_moves:
        move.start()
    f_moves[0].start()
    for dz in range(1, nz):
        b_moves[dz - 1].wait_recv()
        f_moves[dz].start()
    for move in f_moves:
        move.wait_recv()
    rows_ref[...] = held_ref[...].reshape(rows, rows_ref.shape[1])

    chunks, count, piece = gram_ref.shape[:3]

    nt = rows_ref.shape[1] // TILE

    for half, (low, high) in enumerate(tile_halves(nt)):
        starts = [0]
        for i in range(low, high):
            starts.append(starts[-1] + nt - i)

        def tile(t, carry, half=half, low=low, starts=starts):
            at = jnp.minimum(zc * per + t, starts[-1] - 1)
            row, begin = jnp.int32(low), jnp.int32(0)
            for q in range(1, len(starts) - 1):
                row = jnp.where(at >= starts[q], low + q, row)
                begin = jnp.where(at >= starts[q], starts[q], begin)
            i = pl.multiple_of(row * TILE, TILE)
            j = pl.multiple_of((row + at - begin) * TILE, TILE)
            value = tdot(rows_ref[:, pl.ds(i, TILE)], rows_ref[:, pl.ds(j, TILE)], HI) * scale
            gram_ref[:, pl.ds(half * per + t, 1)] = value.reshape(chunks, 1, piece, TILE)
            return carry

        lax.fori_loop(0, per, tile, 0)
    me = y * nx + x
    gram_moves = []
    for dy in range(ny):
        for dx in range(nx):
            if dy or dx:
                to_y, to_x = around(y, ny, dy), around(x, nx, dx)
                at = len(gram_moves)
                gram_moves.append(
                    push(gram_ref.at[to_y * nx + to_x], grams_ref.at[me], g_send.at[at],
                         g_recv.at[at], (to_y, to_x, z, c))
                )
    for move in gram_moves:
        move.start()
    grams_ref[me] = gram_ref[me]
    for move in gram_moves:
        move.wait_recv()
    value = grams_ref[0]
    for q in range(1, chunks):
        value = value + grams_ref[q]
    tiles_ref[...] = value
    for move in (omega_moves + right_moves + left_moves + pair_moves + z_moves + b_moves + f_moves
                 + gram_moves):
        move.wait_send()


def front(gate, left, right, omega, sizes, per, scale):
    ny, nx, nz, nc = sizes
    groups, chunks = nz * nc, ny * nx
    rows, part = left.shape[0] // nx, left.shape[1]
    bond_y, width = right.shape
    step = omega.shape[1]
    k, cols, band = ny * step, nx * width, rows // groups
    piece, count = TILE // chunks, 2 * per
    smem = pl.BlockSpec(memory_space=pltpu.SMEM)
    dma = pltpu.SemaphoreType.DMA
    return pl.pallas_call(
        functools.partial(front_kernel, sizes, per, scale),
        out_shape=(
            jax.ShapeDtypeStruct((rows, cols), BF16),
            jax.ShapeDtypeStruct((rows, k), F32),
            jax.ShapeDtypeStruct((band, k), F32),
            jax.ShapeDtypeStruct((count, piece, TILE), F32),
        ),
        in_specs=[smem, WHOLE, WHOLE, pl.BlockSpec(memory_space=pl.ANY)],
        out_specs=(WHOLE,) * 4,
        scratch_shapes=[
            pltpu.VMEM((nx, part, rows), BF16),
            pltpu.VMEM((groups, nx, part, rows), BF16),
            pltpu.VMEM((nx, bond_y * ny, width), BF16),
            pltpu.VMEM((ny, nx, width, step), BF16),
            pltpu.VMEM((bond_y * ny, rows), BF16),
            pltpu.VMEM((groups, band, k), F32),
            pltpu.VMEM((nz, band, k), F32),
            pltpu.VMEM((nz - 1, band, k), F32),
            pltpu.VMEM((nz - 1, band, k), F32),
            pltpu.VMEM((groups, band, k), F32),
            pltpu.VMEM((chunks, count, piece, TILE), F32),
            pltpu.VMEM((chunks, count, piece, TILE), F32),
            dma, dma((ny - 1,)), dma((ny - 1,)), dma((chunks - 1,)), dma((chunks - 1,)),
            dma((nx * groups - 1,)), dma((nx * groups - 1,)), dma((chunks - 1,)), dma((chunks - 1,)),
            dma((nz,)), dma((nz,)), dma((nz - 1,)), dma((nz - 1,)),
            dma((nz - 1,)), dma((nz - 1,)), dma((nz,)), dma((nz,)),
        ],
        compiler_params=pltpu.CompilerParams(vmem_limit_bytes=VMEM_LIMIT, has_side_effects=True),
        name="front",
    )(gate, left, right, omega)


def cross_kernel(scale, s_ref, theta_ref, out_ref):
    parts, _, width = out_ref.shape
    for at in range(0, s_ref.shape[1], TILE):
        head, rest = split(s_ref[:, at : at + TILE])
        value = (tdot(head, theta_ref[...]) + tdot(rest, theta_ref[...])) * scale
        for x in range(parts):
            out_ref[x, at : at + TILE, :] = value[:, x * width : (x + 1) * width]


def cross(sketch, theta, parts, scale):
    width = theta.shape[1] // parts
    return pl.pallas_call(
        functools.partial(cross_kernel, scale),
        out_shape=jax.ShapeDtypeStruct((parts, sketch.shape[1], width), F32),
        in_specs=[WHOLE, WHOLE],
        out_specs=WHOLE,
        compiler_params=pltpu.CompilerParams(vmem_limit_bytes=VMEM_LIMIT),
        name="cross",
    )(sketch, theta)


def leaf(rows):
    lane = lax.broadcasted_iota(jnp.int32, (8, HALF), 1)
    sub = lax.broadcasted_iota(jnp.int32, (8, HALF), 0)
    rows = list(rows)
    count = len(rows)
    done = []
    for j in range(count):
        base = 8 * j
        here = (lane >= base) & (lane < base + 8)
        part = rows[j]
        cols = [jnp.broadcast_to(part[:, base + k : base + k + 1], (8, HALF)) for k in range(8)]
        part = jnp.where(here, jnp.where(lane - base == sub, 1.0, 0.0), part)
        tri = jnp.zeros((8, HALF), F32)
        for k in range(8):
            at = sub == k
            pivot = jnp.broadcast_to(cols[k][k : k + 1, :], (8, HALF))
            inv = 1.0 / pivot
            row = jnp.broadcast_to(part[k : k + 1, :], (8, HALF))
            tri = jnp.where(at, row * lax.rsqrt(pivot), tri)
            factor = cols[k] * inv
            part = jnp.where(at, row * inv, part - factor * row)
            for m in range(k + 1, 8):
                mrow = jnp.broadcast_to(cols[m][k : k + 1, :], (8, HALF))
                cols[m] = jnp.where(at, mrow * inv, cols[m] - factor * mrow)
        done.append(jnp.where(lane < base + 8, tri, 0.0))
        if j + 1 < count:
            prow = [jnp.broadcast_to(part[k : k + 1, :], (8, HALF)) for k in range(8)]
            for i in range(j + 1, count):
                mine = rows[i]
                terms = [
                    jnp.broadcast_to(mine[:, base + k : base + k + 1], (8, HALF)) * prow[k]
                    for k in range(8)
                ]
                while len(terms) > 1:
                    terms = [terms[q] + terms[q + 1] for q in range(0, len(terms), 2)]
                rows[i] = jnp.where(here, 0.0, mine) - terms[0]
    return done


def stage_kernel(plan, per, *refs):
    first, stop, nt, chunks, has_carry, has_tiles = plan
    refs = list(refs)
    g_ref = refs.pop(0) if has_tiles else None
    carry_ref = refs.pop(0) if has_carry else None
    uh_ref, ul_ref, inv_ref = refs[:3]
    refs = refs[3:]
    last = stop == nt
    out_ref = None if last else refs.pop(0)
    grid_ref, a_ref, l_ref, uab_ref, sem = refs[:5]
    extra_ref = refs[5] if has_carry and has_tiles else None
    m = (nt - first) * TILE
    size = nt - first
    count = stop - first
    t_ref = grid_ref.reshape(m, m)
    copies = []
    if has_tiles:
        groups = g_ref.shape[0] // chunks
        source = g_ref.reshape(chunks, groups, per, TILE // chunks, TILE)
        target = grid_ref if extra_ref is None else extra_ref
        low, high = (first, stop) if not has_carry else (first, nt)
        for at, (i, j) in enumerate((i, j) for i in range(low, high) for j in range(i, nt)):
            rows = pl.ds((i - first) * chunks, chunks)
            cols = pl.ds((j - first) * TILE, TILE)
            copies.append(
                pltpu.make_async_copy(
                    source.at[:, at // per, at % per], target.at[rows, :, cols], sem.at[0]
                )
            )
    if has_carry:
        for i in range(size):
            at = pl.ds(i * TILE, TILE)
            cols = pl.ds(i * TILE, m - i * TILE)
            copies.append(pltpu.make_async_copy(carry_ref.at[at, cols], t_ref.at[at, cols], sem.at[1]))
    for copy in copies:
        copy.start()
    if not has_carry and not last:
        t_ref[count * TILE :, count * TILE :] = jnp.zeros((m - count * TILE,) * 2, F32)
    for copy in copies:
        copy.wait()
    if extra_ref is not None:
        e_ref = extra_ref.reshape(m, m)

        def add_row(r, carry):
            rat = pl.multiple_of(r * TILE, TILE)

            def add(c, carry):
                cat = pl.multiple_of(c * TILE, TILE)
                t_ref[pl.ds(rat, TILE), pl.ds(cat, TILE)] += e_ref[pl.ds(rat, TILE), pl.ds(cat, TILE)]
                return carry

            return lax.fori_loop(r, size, add, carry)

        lax.fori_loop(0, size, add_row, 0)

    def half(p, h, carry):
        base = pl.multiple_of(p * TILE, TILE)
        mid = pl.multiple_of(p * TILE + HALF, HALF)

        @pl.when(h == 0)
        def _():
            a_ref[...] = t_ref[pl.ds(base, HALF), pl.ds(base, HALF)]

        @pl.when(h == 1)
        def _():
            a_ref[...] = t_ref[pl.ds(mid, HALF), pl.ds(mid, HALF)] - tdot(uab_ref[...], uab_ref[...], HI)

        out = leaf([a_ref[8 * i : 8 * i + 8, :] for i in range(HALF // 8)])
        for i, rows in enumerate(out):
            l_ref[8 * i : 8 * i + 8, :] = rows

        @pl.when(h == 0)
        def _():
            inv_ref[p, 0:HALF, 0:HALF] = l_ref[...]
            inv_ref[p, 0:HALF, HALF:] = jnp.zeros((HALF, HALF), F32)
            uab_ref[...] = jnp.dot(
                l_ref[...], t_ref[pl.ds(base, HALF), pl.ds(mid, HALF)], precision=HI
            )

        @pl.when(h == 1)
        def _():
            cross = tdot(uab_ref[...], inv_ref[p, 0:HALF, 0:HALF], HI)
            inv_ref[p, HALF:, 0:HALF] = -jnp.dot(l_ref[...], cross, precision=HI)
            inv_ref[p, HALF:, HALF:] = l_ref[...]

        return carry

    def panel(p, carry):
        base = pl.multiple_of(p * TILE, TILE)
        lax.fori_loop(0, 2, functools.partial(half, p), 0)

        def row_tile(c, carry):
            at = pl.multiple_of(c * TILE, TILE)
            u = jnp.dot(inv_ref[p], t_ref[pl.ds(base, TILE), pl.ds(at, TILE)], precision=HI)
            head, rest = split(u)
            uh_ref[pl.ds(base, TILE), pl.ds(at, TILE)] = head
            ul_ref[pl.ds(base, TILE), pl.ds(at, TILE)] = rest
            return carry

        lax.fori_loop(p + 1, size, row_tile, 0)

        def trail_row(r, carry):
            rat = pl.multiple_of(r * TILE, TILE)
            head = uh_ref[pl.ds(base, TILE), pl.ds(rat, TILE)].T
            rest = ul_ref[pl.ds(base, TILE), pl.ds(rat, TILE)].T

            def trail(c, carry):
                cat = pl.multiple_of(c * TILE, TILE)
                ch = uh_ref[pl.ds(base, TILE), pl.ds(cat, TILE)]
                cl = ul_ref[pl.ds(base, TILE), pl.ds(cat, TILE)]
                update = jnp.dot(head, ch, preferred_element_type=F32) + (
                    jnp.dot(head, cl, preferred_element_type=F32)
                    + jnp.dot(rest, ch, preferred_element_type=F32)
                )
                t_ref[pl.ds(rat, TILE), pl.ds(cat, TILE)] -= update
                return carry

            lax.fori_loop(r, size, trail, 0)
            return carry

        lax.fori_loop(p + 1, size, trail_row, 0)
        return carry

    lax.fori_loop(0, count, panel, 0)
    if out_ref is not None:
        back = []
        for i in range(count, size):
            at = pl.ds((i - count) * TILE, TILE)
            cols = pl.ds((i - count) * TILE, m - i * TILE)
            mine = t_ref.at[pl.ds(i * TILE, TILE), pl.ds(i * TILE, m - i * TILE)]
            back.append(pltpu.make_async_copy(mine, out_ref.at[at, cols], sem.at[0]))
        for copy in back:
            copy.start()
        for copy in back:
            copy.wait()


def stage(first, stop, n, per, chunks, tiles=None, carry=None):
    nt = n // TILE
    m = n - first * TILE
    rows = (stop - first) * TILE
    piece = TILE // chunks
    args = [v for v in (tiles, carry) if v is not None]
    out_shape = [
        jax.ShapeDtypeStruct((rows, m), BF16),
        jax.ShapeDtypeStruct((rows, m), BF16),
        jax.ShapeDtypeStruct((stop - first, TILE, TILE), F32),
    ]
    out_specs = [WHOLE] * 3
    if stop < nt:
        out_shape.append(jax.ShapeDtypeStruct((m - rows, m - rows), F32))
        out_specs.append(pl.BlockSpec(memory_space=pl.ANY))
    scratch = [
        pltpu.VMEM((m // piece, piece, m), F32),
        pltpu.VMEM((HALF, HALF), F32),
        pltpu.VMEM((HALF, HALF), F32),
        pltpu.VMEM((HALF, HALF), F32),
        pltpu.SemaphoreType.DMA((2,)),
    ]
    if len(args) == 2:
        scratch.append(pltpu.VMEM((m // piece, piece, m), F32))
    plan = (first, stop, nt, chunks, carry is not None, tiles is not None)
    return pl.pallas_call(
        functools.partial(stage_kernel, plan, per),
        out_shape=tuple(out_shape),
        in_specs=[pl.BlockSpec(memory_space=pl.ANY)] * len(args),
        out_specs=tuple(out_specs),
        scratch_shapes=scratch,
        compiler_params=pltpu.CompilerParams(vmem_limit_bytes=VMEM_LIMIT),
        cost_estimate=pl.CostEstimate(
            flops=40 * 10**9, bytes_accessed=rows * m * 8, transcendentals=0
        ),
        name=f"stage{first}",
    )(*args)


def solve_kernel(plan, *refs):
    stages = len(plan)
    factors = refs[: 3 * stages]
    s_ref, w_ref, basis_ref, proj_ref, y_ref = refs[3 * stages : 3 * stages + 5]
    held = refs[3 * stages + 5 : 6 * stages + 5]
    sem = refs[6 * stages + 5]
    copies = [
        pltpu.make_async_copy(a, b, sem.at[q]) for q, (a, b) in enumerate(zip(factors, held))
    ]
    for copy in copies:
        copy.start()
    mine, n = s_ref.shape
    nt = n // TILE
    padded = jnp.concatenate([s_ref[...], jnp.zeros((HALF - mine, n), F32)], axis=0)
    y_ref[:, :HALF] = padded.T
    y_ref[:, HALF:] = w_ref[...]
    for q, (first, stop) in enumerate(plan):
        uh_ref, ul_ref, inv_ref = held[3 * q : 3 * q + 3]
        for copy in copies[3 * q : 3 * q + 3]:
            copy.wait()
        for p in range(first, stop):
            rows = slice(p * TILE, (p + 1) * TILE)
            local = slice((p - first) * TILE, (p - first + 1) * TILE)
            y = jnp.dot(inv_ref[p - first], y_ref[rows, :], precision=HI)
            y_ref[rows, :] = y
            proj_ref[rows, :] = y[:, HALF:]
            head, rest = split(y)

            def tail(r, carry):
                at = pl.multiple_of(r * TILE, TILE)
                here = pl.multiple_of((r - first) * TILE, TILE)
                uh = uh_ref[local, pl.ds(here, TILE)]
                ul = ul_ref[local, pl.ds(here, TILE)]
                y_ref[pl.ds(at, TILE), :] -= tdot(uh, head) + (tdot(uh, rest) + tdot(ul, head))
                return carry

            lax.fori_loop(p + 1, nt, tail, 0)
    basis_ref[...] = y_ref[:, :HALF].T[:mine]


def solve(plan, factors, sketch, weights):
    mine, n = sketch.shape
    flat = [v for part in factors for v in part]
    return pl.pallas_call(
        functools.partial(solve_kernel, plan),
        out_shape=(jax.ShapeDtypeStruct((mine, n), F32), jax.ShapeDtypeStruct((n, HALF), F32)),
        in_specs=[pl.BlockSpec(memory_space=pl.ANY)] * len(flat) + [WHOLE, WHOLE],
        out_specs=(WHOLE, WHOLE),
        scratch_shapes=[pltpu.VMEM((n, 2 * HALF), F32)]
        + [pltpu.VMEM(v.shape, v.dtype) for v in flat]
        + [pltpu.SemaphoreType.DMA((len(flat),))],
        compiler_params=pltpu.CompilerParams(vmem_limit_bytes=VMEM_LIMIT),
        name="solve",
    )(*flat, sketch, weights)


CUTS = ((0, 3), (3, 6), (6, 9))


def tile_halves(nt):
    cut = CUTS[0][1]
    return (0, cut), (cut, nt)


def tiles_each(nt, groups):
    counts = [sum(nt - i for i in range(low, high)) for low, high in tile_halves(nt)]
    return -(-max(counts) // groups)


def on_device(left_site, right_site, gate, omega):
    sizes = tuple(lax.axis_size(a) for a in ("row", "x", "z", "core"))
    ny, nx, nz, nc = sizes
    total = left_site.shape[0] * ny
    width = right_site.shape[1]
    n = omega.shape[1] * ny
    chunks = ny * nx
    per = tiles_each(n // TILE, nz * nc)
    theta, sketch_rows, sketch, mine = front(
        gate, left_site, right_site, omega, sizes, per, 1.0 / total
    )
    mine = mine[None]
    everywhere = ("row", "x", "z", "core")
    early = lax.all_gather(mine[:, :per], everywhere, axis=0, tiled=True)
    weights = cross(sketch_rows, theta, nx, 1.0 / math_sqrt(total))
    early, late, weights = lax.optimization_barrier((early, mine[:, per:], weights))
    late = lax.all_gather(late, everywhere, axis=0, tiled=True)
    weights = lax.psum_scatter(weights, "x", scatter_dimension=0, tiled=True)

    *part_a, carry = stage(*CUTS[0], n, per, chunks, tiles=early)
    *part_b, carry = stage(*CUTS[1], n, per, chunks, tiles=late, carry=carry)
    carry, weights = lax.optimization_barrier((carry, weights))
    weights = lax.psum(weights, "row").reshape(n, width)
    part_c = stage(*CUTS[2], n, per, chunks, carry=carry)
    basis, projected = solve(CUTS, (part_a, part_b, part_c), sketch, weights)
    block = n // ny
    return basis, lax.dynamic_slice_in_dim(projected, lax.axis_index("row") * block, block, 0)


def math_sqrt(value):
    return float(np.sqrt(value))


def solution(mesh):
    fine = Mesh(mesh.devices.reshape(4, 4, 4, 2), ("row", "x", "z", "core"))
    col = ("x", "z", "core")
    in_specs = (P("row", col), P("row", col), P(), P(None, "row"))
    out_specs = (P(("row",) + col, None), P("row", col))
    return jax.shard_map(on_device, mesh=fine, in_specs=in_specs, out_specs=out_specs, check_vma=False)
```

```python
import functools

import jax
import jax.numpy as jnp
import numpy as np
from jax import lax
from jax.experimental import pallas as pl
from jax.experimental.pallas import tpu as pltpu
from jax.sharding import Mesh
from jax.sharding import PartitionSpec as P

HI = lax.Precision.HIGHEST
F32, BF16 = jnp.float32, jnp.bfloat16
TILE = 256
HALF = 128
VMEM_LIMIT = 60 << 20
WHOLE = pl.BlockSpec(memory_space=pltpu.VMEM)


def split(x):
    head = x.astype(BF16)
    return head, (x - head.astype(F32)).astype(BF16)


def tdot(a, b, precision=None):
    return lax.dot_general(
        a, b, (((0,), (0,)), ((), ())), preferred_element_type=F32, precision=precision
    )


def near(index, size, step):
    return lax.rem(index + (step + size), size)


def front_kernel(
    sizes, per, scale, cross_scale, gate_ref, left_ref, right_ref, omega_hbm,
    mine_ref, early_ref, late_ref, cross_ref,
    theta_ref, all_left, all_right, all_omega, bond_ref,
    part_ref, pair_ref, relay_ref, got_ref, held_ref,
    ya_ref, ya_relay, ya_got, xa_ref, xa_relay, xa_got,
    xb_ref, xb_relay, xb_got, yb_ref, yb_relay, yb_got,
    local, send, recv,
):
    ny, nx, nz, nc = sizes
    groups = nz * nc
    y, x, z, c = (lax.axis_index(a) for a in ("row", "x", "z", "core"))
    zc = z * nc + c
    twin = (y, x, z, 1 - c)
    part = left_ref.shape[0]
    rows = all_left.shape[3]
    bond_y, width = right_ref.shape
    step = omega_hbm.shape[0]
    band = rows // groups
    moves = []

    def push(src, dst, to):
        at = len(moves)
        move = pltpu.make_async_remote_copy(
            src_ref=src, dst_ref=dst, send_sem=send.at[at], recv_sem=recv.at[at],
            device_id=to, device_id_type=pl.DeviceIdType.MESH,
        )
        moves.append(move)
        return move

    def beside(axis, way):
        place = [y, x, z, c]
        place[axis] = near(place[axis], sizes[axis], way)
        return tuple(place)

    class Gather:
        def __init__(self, axis, block):
            me = (y, x, z)[axis]
            self.below, self.above = near(me, 4, -1), near(me, 4, 1)
            up, down = beside(axis, 1), beside(axis, -1)
            own = block(me, None)
            self.up, self.down = push(own, own, up), push(own, own, down)
            first, second = block(self.below, 0), block(self.above, 1)
            self.far_up, self.far_down = push(first, first, up), push(second, second, down)

        def start(self):
            self.up.start()
            self.down.start()

        def relay(self):
            self.up.wait_recv()
            self.far_up.start()
            self.down.wait_recv()
            self.far_down.start()

        def finish(self):
            self.far_up.wait_recv()
            self.far_down.wait_recv()

    class Reduce:
        def __init__(self, axis, block, relay, got):
            me = (y, x, z)[axis]
            up, down = beside(axis, 1), beside(axis, -1)
            far, above, below = near(me, 4, 2), near(me, 4, 1), near(me, 4, -1)
            self.block, self.me, self.above, self.below, self.far = block, me, above, below, far
            self.relay, self.got = relay, got
            self.far_up = push(block(far, 0), relay.at[0], up)
            self.far_down = push(block(far, 1), relay.at[1], down)
            self.up = push(block(above, None), got.at[0], up)
            self.down = push(block(below, None), got.at[1], down)

        def start(self):
            self.far_up.start()
            self.far_down.start()

        def middle(self):
            self.far_up.wait_recv()
            self.block(self.above, 0)[...] += self.relay[0]
            self.up.start()
            self.far_down.wait_recv()
            self.block(self.below, 1)[...] += self.relay[1]
            self.down.start()

        def finish(self):
            self.up.wait_recv()
            self.down.wait_recv()
            return self.block(self.me, None)[...] + self.got[0] + self.got[1]

    def halved(ref, rows_of, half):
        return ref if half is None else ref.at[pl.ds(half * (rows_of // 2), rows_of // 2)]

    def right_y(slot, half):
        size = bond_y if half is None else bond_y // 2
        begin = slot * bond_y + (0 if half is None else half * size)
        return all_right.at[x, pl.ds(pl.multiple_of(begin, 128), size), :]

    own_omega = [
        pltpu.make_async_copy(
            omega_hbm.at[:, pl.ds(pl.multiple_of((q * groups + zc) * width, width), width)],
            all_omega.at[y, :, pl.ds(q * width, width)], local.at[q],
        )
        for q in range(nx)
    ]
    for move in own_omega:
        move.start()
    all_right[x, pl.ds(pl.multiple_of(y * bond_y, bond_y), bond_y), :] = right_ref[...]
    by_y = Gather(0, right_y)
    by_y.start()
    across = []
    for dx in range(1, nx):
        to_x = near(x, nx, dx)
        src = left_ref.at[:, pl.ds(pl.multiple_of(to_x * rows, rows), rows)]
        across.append(push(src, all_left.at[zc, x], (y, to_x, z, c)))
    for move in across:
        move.start()
    all_left[zc, x] = left_ref[:, pl.ds(pl.multiple_of(x * rows, rows), rows)]
    for move in own_omega:
        move.wait()
    omega_y = Gather(0, lambda slot, half: halved(all_omega.at[slot], step, half))
    omega_y.start()
    by_y.relay()
    for move in across:
        move.wait_recv()
    left_z = Gather(2, lambda slot, half: halved(all_left.at[slot * nc + c], nx, half))
    left_z.start()
    left_twin = [push(all_left.at[near(z, nz, d) * nc + c], all_left.at[near(z, nz, d) * nc + c], twin)
                 for d in (0, -1, 1, 2)]
    left_twin[0].start()
    by_y.finish()
    by_x = Gather(1, lambda slot, half: halved(all_right.at[slot], bond_y * ny, half))
    by_x.start()
    left_z.relay()
    left_twin[1].start()
    left_twin[2].start()
    omega_y.relay()
    left_z.finish()
    left_twin[3].start()
    by_x.relay()
    for move in left_twin:
        move.wait_recv()
    for xs in range(nx):
        for g in range(groups):
            at = (xs * groups + g) * part
            bond_ref[at : at + part, :] = all_left[g, xs]
    by_x.finish()

    left = bond_ref[...]
    row_odd = lax.broadcasted_iota(jnp.int32, (rows, width), 0) % 2 == 1
    col_odd = lax.broadcasted_iota(jnp.int32, (rows, width), 1) % 2 == 1

    def coupling(row_flip, col_flip):
        def entry(s1, s2):
            a, b = s1 ^ row_flip, s2 ^ col_flip
            return gate_ref[2 * s1 + s2, 2 * a + b]

        even = jnp.where(col_odd, entry(0, 1), entry(0, 0))
        odd = jnp.where(col_odd, entry(1, 1), entry(1, 0))
        return jnp.where(row_odd, odd, even)

    for xs in range(nx):
        bare = tdot(left, all_right[xs])
        row_partner = jnp.where(row_odd, pltpu.roll(bare, 1, 0), pltpu.roll(bare, rows - 1, 0))

        def col_partner(v):
            return jnp.where(col_odd, pltpu.roll(v, 1, 1), pltpu.roll(v, width - 1, 1))

        mixed = (coupling(0, 0) * bare + coupling(0, 1) * col_partner(bare)) + (
            coupling(1, 0) * row_partner + coupling(1, 1) * col_partner(row_partner)
        )
        theta_ref[:, xs * width : (xs + 1) * width] = mixed.astype(BF16)
    omega_y.finish()
    theta = theta_ref[...]
    for q in range(ny):
        value = lax.dot_general(
            theta, all_omega[q], (((1,), (1,)), ((), ())), preferred_element_type=F32
        )
        part_ref[:, :, q * step : (q + 1) * step] = value.reshape(groups, band, step)

    order = (2, 1, -1, 0)
    pairs = [
        push(part_ref.at[near(z, nz, d) * nc + 1 - c], pair_ref.at[q], twin) for q, d in enumerate(order)
    ]
    for move in pairs:
        move.start()

    def block_z(slot, half):
        return halved(part_ref.at[slot * nc + c], band, half)

    def add_pair(q):
        pairs[q].wait_recv()
        part_ref[near(z, nz, order[q]) * nc + c] += pair_ref[q]

    sum_z = Reduce(2, block_z, relay_ref, got_ref)
    add_pair(0)
    sum_z.start()
    add_pair(1)
    add_pair(2)
    sum_z.middle()
    add_pair(3)
    total = sum_z.finish()
    held_ref[zc] = total

    rows_z = Gather(2, lambda slot, half: halved(held_ref.at[slot * nc + c], band, half))
    rows_z.start()
    rows_twin = [push(held_ref.at[near(z, nz, d) * nc + c], held_ref.at[near(z, nz, d) * nc + c], twin)
                 for d in (0, -1, 1, 2)]
    rows_twin[0].start()
    mine_ref[...] = total
    rows_z.relay()
    rows_twin[1].start()
    rows_twin[2].start()
    rows_z.finish()
    rows_twin[3].start()
    for move in rows_twin:
        move.wait_recv()
    k = mine_ref.shape[1]
    nt = k // TILE
    piece = early_ref.shape[5]

    def columns(at, count=TILE):
        return held_ref[:, :, pl.ds(at, count)].reshape(rows, count)

    def tiles(half, out):
        low, high = tile_halves(nt)[half]
        starts = [0]
        for i in range(low, high):
            starts.append(starts[-1] + nt - i)

        def tile(t, carry):
            at = jnp.minimum(zc * per + t, starts[-1] - 1)
            row, begin = jnp.int32(low), jnp.int32(0)
            for q in range(1, len(starts) - 1):
                row = jnp.where(at >= starts[q], low + q, row)
                begin = jnp.where(at >= starts[q], starts[q], begin)
            i = pl.multiple_of(row * TILE, TILE)
            j = pl.multiple_of((row + at - begin) * TILE, TILE)
            value = tdot(columns(i), columns(j), HI) * scale
            for q in range(ny):
                for r in range(nx):
                    at = (q * nx + r) * piece
                    spot = (q, r) if half == 0 else (r, q)
                    out[spot[0], spot[1], pl.ds(t, 1)] = value[at : at + piece].reshape(1, piece, TILE)
            return carry

        lax.fori_loop(0, per, tile, 0)

    def lower_rows(ref, slot, half):
        if half is None:
            return ref.at[slot]
        return ref.at[slot, :, pl.ds(half * (piece // 2), piece // 2)]

    first_a = Reduce(0, lambda s, h: halved(ya_ref.at[s], nx, h), ya_relay, ya_got)
    first_b = Reduce(1, lambda s, h: halved(xb_ref.at[s], ny, h), xb_relay, xb_got)
    tiles(0, ya_ref)
    first_a.start()
    tiles(1, xb_ref)
    first_a.middle()
    first_b.start()
    xa_ref[...] = first_a.finish()
    then_a = Reduce(1, lambda s, h: lower_rows(xa_ref, s, h), xa_relay, xa_got)
    then_a.start()
    first_b.middle()
    then_a.middle()
    yb_ref[...] = first_b.finish()
    then_b = Reduce(0, lambda s, h: lower_rows(yb_ref, s, h), yb_relay, yb_got)
    then_b.start()
    early_ref[y, x, z, c] = then_a.finish()

    spots = ((2, 0, 1), (0, 1, 2), (1, 2, 0))
    here = (y, x, z)

    def plane(t, phase):
        axes = spots[t]
        along = axes[phase]

        def block(slot, half):
            index = [here[0], here[1], here[2]]
            for done in axes[:phase]:
                index[done] = slice(None)
            index[along] = slot
            if half is not None and phase == 0:
                rows_at = pl.ds(half * (piece // 2), piece // 2)
                return early_ref.at[index[0], index[1], index[2], c, t, rows_at]
            if half is not None:
                index[axes[0]] = pl.ds(2 * half, 2)
            return early_ref.at[index[0], index[1], index[2], c, t]

        return along, block

    rings = []
    for t in range(per):
        along, block = plane(t, 0)
        rings.append(Gather(along, block))
        rings[t].start()
    then_b.middle()
    for ring in rings:
        ring.relay()
    late_ref[...] = then_b.finish()
    second = []
    for t in range(per):
        rings[t].finish()
        along, block = plane(t, 1)
        second.append(Gather(along, block))
        second[t].start()
    for ring in second:
        ring.relay()
    third, to_twin = [], []
    for t in range(per):
        second[t].finish()
        along, block = plane(t, 2)
        third.append(Gather(along, block))
        third[t].start()
        me = here[along]
        group = []
        for d in (0, -1, 1, 2):
            ref = block(near(me, 4, d), None)
            group.append(push(ref, ref, twin))
        to_twin.append(group)
        group[0].start()

    theta = theta_ref[...]
    for at in range(0, k, TILE):
        head, rest = split(columns(at))
        value = (tdot(head, theta) + tdot(rest, theta)) * cross_scale
        for q in range(nx):
            cross_ref[q, at : at + TILE, :] = value[:, q * width : (q + 1) * width]

    for t in range(per):
        third[t].relay()
        to_twin[t][1].start()
        to_twin[t][2].start()
    for t in range(per):
        third[t].finish()
        to_twin[t][3].start()
    for group in to_twin:
        for move in group:
            move.wait_recv()
    for move in moves:
        move.wait_send()


def front(gate, left, right, omega, sizes, per, scale, cross_scale):
    ny, nx, nz, nc = sizes
    groups, chunks = nz * nc, ny * nx
    part, rows = left.shape[0], left.shape[1] // nx
    bond_y, width = right.shape
    step = omega.shape[0]
    k, cols, band = ny * step, nx * width, rows // groups
    piece = TILE // chunks
    smem = pl.BlockSpec(memory_space=pltpu.SMEM)
    dma = pltpu.SemaphoreType.DMA
    vmem = pltpu.VMEM

    def sums(first, second):
        return [
            vmem((first, second, per, piece, TILE), F32),
            vmem((2, second // 2, per, piece, TILE), F32),
            vmem((2, second, per, piece, TILE), F32),
            vmem((second, per, piece, TILE), F32),
            vmem((2, per, piece // 2, TILE), F32),
            vmem((2, per, piece, TILE), F32),
        ]

    return pl.pallas_call(
        functools.partial(front_kernel, sizes, per, scale, cross_scale),
        out_shape=(
            jax.ShapeDtypeStruct((band, k), F32),
            jax.ShapeDtypeStruct((ny, nx, nz, nc, per, piece, TILE), F32),
            jax.ShapeDtypeStruct((per, piece, TILE), F32),
            jax.ShapeDtypeStruct((nx, k, width), F32),
        ),
        in_specs=[smem, WHOLE, WHOLE, pl.BlockSpec(memory_space=pl.ANY)],
        out_specs=(WHOLE,) * 4,
        scratch_shapes=[
            vmem((rows, cols), BF16),
            vmem((groups, nx, part, rows), BF16),
            vmem((nx, bond_y * ny, width), BF16),
            vmem((ny, step, cols), BF16),
            vmem((bond_y * ny, rows), BF16),
            vmem((groups, band, k), F32),
            vmem((nz, band, k), F32),
            vmem((2, band // 2, k), F32),
            vmem((2, band, k), F32),
            vmem((groups, band, k), F32),
        ]
        + sums(ny, nx)
        + sums(nx, ny)
        + [dma((nx,)), dma((128,)), dma((128,))],
        compiler_params=pltpu.CompilerParams(vmem_limit_bytes=VMEM_LIMIT, has_side_effects=True),
        name="front",
    )(gate, left, right, omega)


def leaf(rows):
    lane = lax.broadcasted_iota(jnp.int32, (8, HALF), 1)
    sub = lax.broadcasted_iota(jnp.int32, (8, HALF), 0)
    rows = list(rows)
    count = len(rows)
    done = []
    for j in range(count):
        base = 8 * j
        here = (lane >= base) & (lane < base + 8)
        part = rows[j]
        cols = [jnp.broadcast_to(part[:, base + k : base + k + 1], (8, HALF)) for k in range(8)]
        part = jnp.where(here, jnp.where(lane - base == sub, 1.0, 0.0), part)
        tri = jnp.zeros((8, HALF), F32)
        for k in range(8):
            at = sub == k
            pivot = jnp.broadcast_to(cols[k][k : k + 1, :], (8, HALF))
            inv = 1.0 / pivot
            row = jnp.broadcast_to(part[k : k + 1, :], (8, HALF))
            tri = jnp.where(at, row * lax.rsqrt(pivot), tri)
            factor = cols[k] * inv
            part = jnp.where(at, row * inv, part - factor * row)
            for m in range(k + 1, 8):
                mrow = jnp.broadcast_to(cols[m][k : k + 1, :], (8, HALF))
                cols[m] = jnp.where(at, mrow * inv, cols[m] - factor * mrow)
        done.append(jnp.where(lane < base + 8, tri, 0.0))
        if j + 1 < count:
            prow = [jnp.broadcast_to(part[k : k + 1, :], (8, HALF)) for k in range(8)]
            for i in range(j + 1, count):
                mine = rows[i]
                terms = [
                    jnp.broadcast_to(mine[:, base + k : base + k + 1], (8, HALF)) * prow[k]
                    for k in range(8)
                ]
                while len(terms) > 1:
                    terms = [terms[q] + terms[q + 1] for q in range(0, len(terms), 2)]
                rows[i] = jnp.where(here, 0.0, mine) - terms[0]
    return done


def stage_kernel(plan, per, *refs):
    first, stop, nt, chunks, has_carry, has_tiles = plan
    refs = list(refs)
    g_ref = refs.pop(0) if has_tiles else None
    carry_ref = refs.pop(0) if has_carry else None
    uh_ref, ul_ref, inv_ref = refs[:3]
    refs = refs[3:]
    last = stop == nt
    out_ref = None if last else refs.pop(0)
    grid_ref, a_ref, l_ref, uab_ref, sem = refs[:5]
    extra_ref = refs[5] if has_carry and has_tiles else None
    m = (nt - first) * TILE
    size = nt - first
    count = stop - first
    t_ref = grid_ref.reshape(m, m)
    copies = []
    if has_tiles:
        groups = g_ref.shape[0] // chunks
        source = g_ref.reshape(chunks, groups, per, TILE // chunks, TILE)
        target = grid_ref if extra_ref is None else extra_ref
        low, high = (first, stop) if not has_carry else (first, nt)
        for at, (i, j) in enumerate((i, j) for i in range(low, high) for j in range(i, nt)):
            rows = pl.ds((i - first) * chunks, chunks)
            cols = pl.ds((j - first) * TILE, TILE)
            copies.append(
                pltpu.make_async_copy(
                    source.at[:, at // per, at % per], target.at[rows, :, cols], sem.at[0]
                )
            )
    if has_carry:
        for i in range(size):
            at = pl.ds(i * TILE, TILE)
            cols = pl.ds(i * TILE, m - i * TILE)
            copies.append(pltpu.make_async_copy(carry_ref.at[at, cols], t_ref.at[at, cols], sem.at[1]))
    for copy in copies:
        copy.start()
    if not has_carry and not last:
        t_ref[count * TILE :, count * TILE :] = jnp.zeros((m - count * TILE,) * 2, F32)
    for copy in copies:
        copy.wait()
    if extra_ref is not None:
        e_ref = extra_ref.reshape(m, m)

        def add_row(r, carry):
            rat = pl.multiple_of(r * TILE, TILE)

            def add(c, carry):
                cat = pl.multiple_of(c * TILE, TILE)
                t_ref[pl.ds(rat, TILE), pl.ds(cat, TILE)] += e_ref[pl.ds(rat, TILE), pl.ds(cat, TILE)]
                return carry

            return lax.fori_loop(r, size, add, carry)

        lax.fori_loop(0, size, add_row, 0)

    def half(p, h, carry):
        base = pl.multiple_of(p * TILE, TILE)
        mid = pl.multiple_of(p * TILE + HALF, HALF)

        @pl.when(h == 0)
        def _():
            a_ref[...] = t_ref[pl.ds(base, HALF), pl.ds(base, HALF)]

        @pl.when(h == 1)
        def _():
            a_ref[...] = t_ref[pl.ds(mid, HALF), pl.ds(mid, HALF)] - tdot(uab_ref[...], uab_ref[...], HI)

        out = leaf([a_ref[8 * i : 8 * i + 8, :] for i in range(HALF // 8)])
        for i, rows in enumerate(out):
            l_ref[8 * i : 8 * i + 8, :] = rows

        @pl.when(h == 0)
        def _():
            inv_ref[p, 0:HALF, 0:HALF] = l_ref[...]
            inv_ref[p, 0:HALF, HALF:] = jnp.zeros((HALF, HALF), F32)
            uab_ref[...] = jnp.dot(
                l_ref[...], t_ref[pl.ds(base, HALF), pl.ds(mid, HALF)], precision=HI
            )

        @pl.when(h == 1)
        def _():
            cross = tdot(uab_ref[...], inv_ref[p, 0:HALF, 0:HALF], HI)
            inv_ref[p, HALF:, 0:HALF] = -jnp.dot(l_ref[...], cross, precision=HI)
            inv_ref[p, HALF:, HALF:] = l_ref[...]

        return carry

    def panel(p, carry):
        base = pl.multiple_of(p * TILE, TILE)
        lax.fori_loop(0, 2, functools.partial(half, p), 0)

        def row_tile(c, carry):
            at = pl.multiple_of(c * TILE, TILE)
            u = jnp.dot(inv_ref[p], t_ref[pl.ds(base, TILE), pl.ds(at, TILE)], precision=HI)
            head, rest = split(u)
            uh_ref[pl.ds(base, TILE), pl.ds(at, TILE)] = head
            ul_ref[pl.ds(base, TILE), pl.ds(at, TILE)] = rest
            return carry

        lax.fori_loop(p + 1, size, row_tile, 0)

        def trail_row(r, carry):
            rat = pl.multiple_of(r * TILE, TILE)
            head = uh_ref[pl.ds(base, TILE), pl.ds(rat, TILE)].T
            rest = ul_ref[pl.ds(base, TILE), pl.ds(rat, TILE)].T

            def trail(c, carry):
                cat = pl.multiple_of(c * TILE, TILE)
                ch = uh_ref[pl.ds(base, TILE), pl.ds(cat, TILE)]
                cl = ul_ref[pl.ds(base, TILE), pl.ds(cat, TILE)]
                update = jnp.dot(head, ch, preferred_element_type=F32) + (
                    jnp.dot(head, cl, preferred_element_type=F32)
                    + jnp.dot(rest, ch, preferred_element_type=F32)
                )
                t_ref[pl.ds(rat, TILE), pl.ds(cat, TILE)] -= update
                return carry

            lax.fori_loop(r, size, trail, 0)
            return carry

        lax.fori_loop(p + 1, size, trail_row, 0)
        return carry

    lax.fori_loop(0, count, panel, 0)
    if out_ref is not None:
        back = []
        for i in range(count, size):
            at = pl.ds((i - count) * TILE, TILE)
            cols = pl.ds((i - count) * TILE, m - i * TILE)
            mine = t_ref.at[pl.ds(i * TILE, TILE), pl.ds(i * TILE, m - i * TILE)]
            back.append(pltpu.make_async_copy(mine, out_ref.at[at, cols], sem.at[0]))
        for copy in back:
            copy.start()
        for copy in back:
            copy.wait()


def stage(first, stop, n, per, chunks, tiles=None, carry=None):
    nt = n // TILE
    m = n - first * TILE
    rows = (stop - first) * TILE
    piece = TILE // chunks
    args = [v for v in (tiles, carry) if v is not None]
    out_shape = [
        jax.ShapeDtypeStruct((rows, m), BF16),
        jax.ShapeDtypeStruct((rows, m), BF16),
        jax.ShapeDtypeStruct((stop - first, TILE, TILE), F32),
    ]
    out_specs = [WHOLE] * 3
    if stop < nt:
        out_shape.append(jax.ShapeDtypeStruct((m - rows, m - rows), F32))
        out_specs.append(pl.BlockSpec(memory_space=pl.ANY))
    scratch = [
        pltpu.VMEM((m // piece, piece, m), F32),
        pltpu.VMEM((HALF, HALF), F32),
        pltpu.VMEM((HALF, HALF), F32),
        pltpu.VMEM((HALF, HALF), F32),
        pltpu.SemaphoreType.DMA((2,)),
    ]
    if len(args) == 2:
        scratch.append(pltpu.VMEM((m // piece, piece, m), F32))
    plan = (first, stop, nt, chunks, carry is not None, tiles is not None)
    return pl.pallas_call(
        functools.partial(stage_kernel, plan, per),
        out_shape=tuple(out_shape),
        in_specs=[pl.BlockSpec(memory_space=pl.ANY)] * len(args),
        out_specs=tuple(out_specs),
        scratch_shapes=scratch,
        compiler_params=pltpu.CompilerParams(vmem_limit_bytes=VMEM_LIMIT),
        cost_estimate=pl.CostEstimate(
            flops=40 * 10**9, bytes_accessed=rows * m * 8, transcendentals=0
        ),
        name=f"stage{first}",
    )(*args)


def solve_kernel(plan, *refs):
    stages = len(plan)
    factors = refs[: 3 * stages]
    s_ref, w_ref, basis_ref, proj_ref, y_ref = refs[3 * stages : 3 * stages + 5]
    held = refs[3 * stages + 5 : 6 * stages + 5]
    sem = refs[6 * stages + 5]
    copies = [
        pltpu.make_async_copy(a, b, sem.at[q]) for q, (a, b) in enumerate(zip(factors, held))
    ]
    for copy in copies:
        copy.start()
    mine, n = s_ref.shape
    nt = n // TILE
    padded = jnp.concatenate([s_ref[...], jnp.zeros((HALF - mine, n), F32)], axis=0)
    y_ref[:, :HALF] = padded.T
    y_ref[:, HALF:] = w_ref[...]
    for q, (first, stop) in enumerate(plan):
        uh_ref, ul_ref, inv_ref = held[3 * q : 3 * q + 3]
        for copy in copies[3 * q : 3 * q + 3]:
            copy.wait()
        for p in range(first, stop):
            rows = slice(p * TILE, (p + 1) * TILE)
            local = slice((p - first) * TILE, (p - first + 1) * TILE)
            y = jnp.dot(inv_ref[p - first], y_ref[rows, :], precision=HI)
            y_ref[rows, :] = y
            proj_ref[rows, :] = y[:, HALF:]
            head, rest = split(y)

            def tail(r, carry):
                at = pl.multiple_of(r * TILE, TILE)
                here = pl.multiple_of((r - first) * TILE, TILE)
                uh = uh_ref[local, pl.ds(here, TILE)]
                ul = ul_ref[local, pl.ds(here, TILE)]
                y_ref[pl.ds(at, TILE), :] -= tdot(uh, head) + (tdot(uh, rest) + tdot(ul, head))
                return carry

            lax.fori_loop(p + 1, nt, tail, 0)
    basis_ref[...] = y_ref[:, :HALF].T[:mine]


def solve(plan, factors, sketch, weights):
    mine, n = sketch.shape
    flat = [v for part in factors for v in part]
    return pl.pallas_call(
        functools.partial(solve_kernel, plan),
        out_shape=(jax.ShapeDtypeStruct((mine, n), F32), jax.ShapeDtypeStruct((n, HALF), F32)),
        in_specs=[pl.BlockSpec(memory_space=pl.ANY)] * len(flat) + [WHOLE, WHOLE],
        out_specs=(WHOLE, WHOLE),
        scratch_shapes=[pltpu.VMEM((n, 2 * HALF), F32)]
        + [pltpu.VMEM(v.shape, v.dtype) for v in flat]
        + [pltpu.SemaphoreType.DMA((len(flat),))],
        compiler_params=pltpu.CompilerParams(vmem_limit_bytes=VMEM_LIMIT),
        name="solve",
    )(*flat, sketch, weights)


CUTS = ((0, 3), (3, 6), (6, 9))


def tile_halves(nt):
    cut = CUTS[0][1]
    return (0, cut), (cut, nt)


def tiles_each(nt, groups):
    counts = [sum(nt - i for i in range(low, high)) for low, high in tile_halves(nt)]
    return -(-max(counts) // groups)


def on_device(left_site, right_site, gate, omega):
    sizes = tuple(lax.axis_size(a) for a in ("row", "x", "z", "core"))
    ny, nx, nz, nc = sizes
    total = left_site.shape[0] * ny
    width = right_site.shape[1]
    n = omega.shape[1] * ny
    chunks = ny * nx
    per = tiles_each(n // TILE, nz * nc)
    sketch, early, late, weights = front(
        gate, left_site.T, right_site, omega.T, sizes, per, 1.0 / total, 1.0 / math_sqrt(total)
    )
    early = early.reshape((ny * nx * nz * nc,) + early.shape[4:])
    late = lax.all_gather(late[None], ("row", "x", "z", "core"), axis=0, tiled=True)
    weights = lax.psum_scatter(weights, "x", scatter_dimension=0, tiled=True)

    *part_a, carry = stage(*CUTS[0], n, per, chunks, tiles=early)
    *part_b, carry = stage(*CUTS[1], n, per, chunks, tiles=late, carry=carry)
    carry, weights = lax.optimization_barrier((carry, weights))
    weights = lax.psum(weights, "row").reshape(n, width)
    part_c = stage(*CUTS[2], n, per, chunks, carry=carry)
    basis, projected = solve(CUTS, (part_a, part_b, part_c), sketch, weights)
    block = n // ny
    return basis, lax.dynamic_slice_in_dim(projected, lax.axis_index("row") * block, block, 0)


def math_sqrt(value):
    return float(np.sqrt(value))


def solution(mesh):
    fine = Mesh(mesh.devices.reshape(4, 4, 4, 2), ("row", "x", "z", "core"))
    col = ("x", "z", "core")
    in_specs = (P("row", col), P("row", col), P(), P(None, "row"))
    out_specs = (P(("row",) + col, None), P("row", col))
    return jax.shard_map(on_device, mesh=fine, in_specs=in_specs, out_specs=out_specs, check_vma=False)
```

```python
import functools

import jax
import jax.numpy as jnp
import numpy as np
from jax import lax
from jax.experimental import pallas as pl
from jax.experimental.pallas import tpu as pltpu
from jax.sharding import Mesh
from jax.sharding import PartitionSpec as P

HI = lax.Precision.HIGHEST
F32, BF16 = jnp.float32, jnp.bfloat16
TILE = 256
HALF = 128
VMEM_LIMIT = 60 << 20
WHOLE = pl.BlockSpec(memory_space=pltpu.VMEM)


def split(x):
    head = x.astype(BF16)
    return head, (x - head.astype(F32)).astype(BF16)


def tdot(a, b, precision=None):
    return lax.dot_general(
        a, b, (((0,), (0,)), ((), ())), preferred_element_type=F32, precision=precision
    )


def near(index, size, step):
    return lax.rem(index + (step + size), size)


def front_kernel(
    sizes, per, scale, cross_scale, gate_ref, left_ref, right_ref, omega_hbm,
    mine_ref, early_ref, late_ref, cross_ref,
    theta_ref, all_left, all_right, all_omega, bond_ref,
    part_ref, pair_ref, relay_ref, got_ref, held_ref,
    ya_ref, ya_relay, ya_got, xa_ref, xa_relay, xa_got,
    xb_ref, xb_relay, xb_got, yb_ref, yb_relay, yb_got,
    local, send, recv,
):
    ny, nx, nz, nc = sizes
    groups = nz * nc
    y, x, z, c = (lax.axis_index(a) for a in ("row", "x", "z", "core"))
    zc = z * nc + c
    twin = (y, x, z, 1 - c)
    part = left_ref.shape[0]
    rows = all_left.shape[3]
    bond_y, width = right_ref.shape
    step = omega_hbm.shape[0]
    band = rows // groups
    moves = []

    def push(src, dst, to):
        at = len(moves)
        move = pltpu.make_async_remote_copy(
            src_ref=src, dst_ref=dst, send_sem=send.at[at], recv_sem=recv.at[at],
            device_id=to, device_id_type=pl.DeviceIdType.MESH,
        )
        moves.append(move)
        return move

    def beside(axis, way):
        place = [y, x, z, c]
        place[axis] = near(place[axis], sizes[axis], way)
        return tuple(place)

    class Gather:
        def __init__(self, axis, block):
            me = (y, x, z)[axis]
            self.below, self.above = near(me, 4, -1), near(me, 4, 1)
            up, down = beside(axis, 1), beside(axis, -1)
            own = block(me, None)
            self.up, self.down = push(own, own, up), push(own, own, down)
            first, second = block(self.below, 0), block(self.above, 1)
            self.far_up, self.far_down = push(first, first, up), push(second, second, down)

        def start(self):
            self.up.start()
            self.down.start()

        def relay(self):
            self.up.wait_recv()
            self.far_up.start()
            self.down.wait_recv()
            self.far_down.start()

        def finish(self):
            self.far_up.wait_recv()
            self.far_down.wait_recv()

    class Reduce:
        def __init__(self, axis, block, relay, got):
            me = (y, x, z)[axis]
            up, down = beside(axis, 1), beside(axis, -1)
            far, above, below = near(me, 4, 2), near(me, 4, 1), near(me, 4, -1)
            self.block, self.me, self.above, self.below, self.far = block, me, above, below, far
            self.relay, self.got = relay, got
            self.far_up = push(block(far, 0), relay.at[0], up)
            self.far_down = push(block(far, 1), relay.at[1], down)
            self.up = push(block(above, None), got.at[0], up)
            self.down = push(block(below, None), got.at[1], down)

        def start(self):
            self.far_up.start()
            self.far_down.start()

        def middle(self):
            self.far_up.wait_recv()
            self.block(self.above, 0)[...] += self.relay[0]
            self.up.start()
            self.far_down.wait_recv()
            self.block(self.below, 1)[...] += self.relay[1]
            self.down.start()

        def finish(self):
            self.up.wait_recv()
            self.down.wait_recv()
            return self.block(self.me, None)[...] + self.got[0] + self.got[1]

    def halved(ref, rows_of, half):
        return ref if half is None else ref.at[pl.ds(half * (rows_of // 2), rows_of // 2)]

    def right_y(slot, half):
        size = bond_y if half is None else bond_y // 2
        begin = slot * bond_y + (0 if half is None else half * size)
        return all_right.at[x, pl.ds(pl.multiple_of(begin, 128), size), :]

    own_omega = [
        pltpu.make_async_copy(
            omega_hbm.at[:, pl.ds(pl.multiple_of((q * groups + zc) * width, width), width)],
            all_omega.at[y, :, pl.ds(q * width, width)], local.at[q],
        )
        for q in range(nx)
    ]
    for move in own_omega:
        move.start()
    all_right[x, pl.ds(pl.multiple_of(y * bond_y, bond_y), bond_y), :] = right_ref[...]
    by_y = Gather(0, right_y)
    by_y.start()
    across = []
    for dx in range(1, nx):
        to_x = near(x, nx, dx)
        src = left_ref.at[:, pl.ds(pl.multiple_of(to_x * rows, rows), rows)]
        across.append(push(src, all_left.at[zc, x], (y, to_x, z, c)))
    for move in across:
        move.start()
    all_left[zc, x] = left_ref[:, pl.ds(pl.multiple_of(x * rows, rows), rows)]

    def right_x(row):
        at = pl.ds(pl.multiple_of(row * bond_y, bond_y), bond_y)

        def block(slot, half):
            if half is None:
                return all_right.at[slot, at, :]
            size = bond_y // 2
            return all_right.at[slot, pl.ds(pl.multiple_of(row * bond_y + half * size, size), size), :]

        return Gather(1, block)

    by_x = [right_x(near(y, ny, d)) for d in (0, -1, 1, 2)]
    by_x[0].start()
    by_y.up.wait_recv()
    by_y.far_up.start()
    by_x[1].start()
    by_y.down.wait_recv()
    by_y.far_down.start()
    by_x[2].start()
    for move in own_omega:
        move.wait()
    omega_y = Gather(0, lambda slot, half: halved(all_omega.at[slot], step, half))
    omega_y.start()
    for move in across:
        move.wait_recv()
    left_z = Gather(2, lambda slot, half: halved(all_left.at[slot * nc + c], nx, half))
    left_z.start()
    left_twin = [push(all_left.at[near(z, nz, d) * nc + c], all_left.at[near(z, nz, d) * nc + c], twin)
                 for d in (0, -1, 1, 2)]
    left_twin[0].start()
    by_x[0].relay()
    by_y.finish()
    by_x[3].start()
    left_z.relay()
    left_twin[1].start()
    left_twin[2].start()
    by_x[1].relay()
    by_x[2].relay()
    left_z.finish()
    left_twin[3].start()
    by_x[3].relay()
    omega_y.relay()
    for move in left_twin:
        move.wait_recv()
    for xs in range(nx):
        for g in range(groups):
            at = (xs * groups + g) * part
            bond_ref[at : at + part, :] = all_left[g, xs]
    for ring in by_x:
        ring.finish()

    left = bond_ref[...]
    row_odd = lax.broadcasted_iota(jnp.int32, (rows, width), 0) % 2 == 1
    col_odd = lax.broadcasted_iota(jnp.int32, (rows, width), 1) % 2 == 1

    def coupling(row_flip, col_flip):
        def entry(s1, s2):
            a, b = s1 ^ row_flip, s2 ^ col_flip
            return gate_ref[2 * s1 + s2, 2 * a + b]

        even = jnp.where(col_odd, entry(0, 1), entry(0, 0))
        odd = jnp.where(col_odd, entry(1, 1), entry(1, 0))
        return jnp.where(row_odd, odd, even)

    for xs in range(nx):
        bare = tdot(left, all_right[xs])
        row_partner = jnp.where(row_odd, pltpu.roll(bare, 1, 0), pltpu.roll(bare, rows - 1, 0))

        def col_partner(v):
            return jnp.where(col_odd, pltpu.roll(v, 1, 1), pltpu.roll(v, width - 1, 1))

        mixed = (coupling(0, 0) * bare + coupling(0, 1) * col_partner(bare)) + (
            coupling(1, 0) * row_partner + coupling(1, 1) * col_partner(row_partner)
        )
        theta_ref[:, xs * width : (xs + 1) * width] = mixed.astype(BF16)
    omega_y.finish()
    theta = theta_ref[...]
    for q in range(ny):
        value = lax.dot_general(
            theta, all_omega[q], (((1,), (1,)), ((), ())), preferred_element_type=F32
        )
        part_ref[:, :, q * step : (q + 1) * step] = value.reshape(groups, band, step)

    order = (2, 1, -1, 0)
    pairs = [
        push(part_ref.at[near(z, nz, d) * nc + 1 - c], pair_ref.at[q], twin) for q, d in enumerate(order)
    ]
    for move in pairs:
        move.start()

    def block_z(slot, half):
        return halved(part_ref.at[slot * nc + c], band, half)

    def add_pair(q):
        pairs[q].wait_recv()
        part_ref[near(z, nz, order[q]) * nc + c] += pair_ref[q]

    sum_z = Reduce(2, block_z, relay_ref, got_ref)
    add_pair(0)
    sum_z.start()
    add_pair(1)
    add_pair(2)
    sum_z.middle()
    add_pair(3)
    total = sum_z.finish()
    held_ref[zc] = total

    rows_z = Gather(2, lambda slot, half: halved(held_ref.at[slot * nc + c], band, half))
    rows_z.start()
    rows_twin = [push(held_ref.at[near(z, nz, d) * nc + c], held_ref.at[near(z, nz, d) * nc + c], twin)
                 for d in (0, -1, 1, 2)]
    rows_twin[0].start()
    mine_ref[...] = total
    rows_z.relay()
    rows_twin[1].start()
    rows_twin[2].start()
    rows_z.finish()
    rows_twin[3].start()
    for move in rows_twin:
        move.wait_recv()
    k = mine_ref.shape[1]
    nt = k // TILE
    piece = early_ref.shape[5]

    def columns(at, count=TILE):
        return held_ref[:, :, pl.ds(at, count)].reshape(rows, count)

    def tiles(half, out):
        low, high = tile_halves(nt)[half]
        starts = [0]
        for i in range(low, high):
            starts.append(starts[-1] + nt - i)

        def tile(t, carry):
            at = jnp.minimum(zc * per + t, starts[-1] - 1)
            row, begin = jnp.int32(low), jnp.int32(0)
            for q in range(1, len(starts) - 1):
                row = jnp.where(at >= starts[q], low + q, row)
                begin = jnp.where(at >= starts[q], starts[q], begin)
            i = pl.multiple_of(row * TILE, TILE)
            j = pl.multiple_of((row + at - begin) * TILE, TILE)
            value = tdot(columns(i), columns(j), HI) * scale
            for q in range(ny):
                for r in range(nx):
                    at = (q * nx + r) * piece
                    spot = (q, r) if half == 0 else (r, q)
                    out[spot[0], spot[1], pl.ds(t, 1)] = value[at : at + piece].reshape(1, piece, TILE)
            return carry

        lax.fori_loop(0, per, tile, 0)

    def lower_rows(ref, slot, half):
        if half is None:
            return ref.at[slot]
        return ref.at[slot, :, pl.ds(half * (piece // 2), piece // 2)]

    first_a = Reduce(0, lambda s, h: halved(ya_ref.at[s], nx, h), ya_relay, ya_got)
    first_b = Reduce(1, lambda s, h: halved(xb_ref.at[s], ny, h), xb_relay, xb_got)
    tiles(0, ya_ref)
    first_a.start()
    tiles(1, xb_ref)
    first_a.middle()
    first_b.start()
    xa_ref[...] = first_a.finish()
    then_a = Reduce(1, lambda s, h: lower_rows(xa_ref, s, h), xa_relay, xa_got)
    then_a.start()
    first_b.middle()
    then_a.middle()
    yb_ref[...] = first_b.finish()
    then_b = Reduce(0, lambda s, h: lower_rows(yb_ref, s, h), yb_relay, yb_got)
    then_b.start()
    early_ref[y, x, z, c] = then_a.finish()

    spots = ((2, 0, 1), (0, 1, 2), (1, 2, 0))
    here = (y, x, z)

    def plane(t, phase):
        axes = spots[t]
        along = axes[phase]

        def block(slot, half):
            index = [here[0], here[1], here[2]]
            for done in axes[:phase]:
                index[done] = slice(None)
            index[along] = slot
            if half is not None and phase == 0:
                rows_at = pl.ds(half * (piece // 2), piece // 2)
                return early_ref.at[index[0], index[1], index[2], c, t, rows_at]
            if half is not None:
                index[axes[0]] = pl.ds(2 * half, 2)
            return early_ref.at[index[0], index[1], index[2], c, t]

        return along, block

    rings = []
    for t in range(per):
        along, block = plane(t, 0)
        rings.append(Gather(along, block))
        rings[t].start()
    then_b.middle()
    for ring in rings:
        ring.relay()
    late_ref[...] = then_b.finish()
    second = []
    for t in range(per):
        rings[t].finish()
        along, block = plane(t, 1)
        second.append(Gather(along, block))
        second[t].start()
    for ring in second:
        ring.relay()
    third, to_twin = [], []
    for t in range(per):
        second[t].finish()
        along, block = plane(t, 2)
        third.append(Gather(along, block))
        third[t].start()
        me = here[along]
        group = []
        for d in (0, -1, 1, 2):
            ref = block(near(me, 4, d), None)
            group.append(push(ref, ref, twin))
        to_twin.append(group)
        group[0].start()

    theta = theta_ref[...]
    for at in range(0, k, TILE):
        head, rest = split(columns(at))
        value = (tdot(head, theta) + tdot(rest, theta)) * cross_scale
        for q in range(nx):
            cross_ref[q, at : at + TILE, :] = value[:, q * width : (q + 1) * width]

    for t in range(per):
        third[t].relay()
        to_twin[t][1].start()
        to_twin[t][2].start()
    for t in range(per):
        third[t].finish()
        to_twin[t][3].start()
    for group in to_twin:
        for move in group:
            move.wait_recv()
    for move in moves:
        move.wait_send()


def front(gate, left, right, omega, sizes, per, scale, cross_scale):
    ny, nx, nz, nc = sizes
    groups, chunks = nz * nc, ny * nx
    part, rows = left.shape[0], left.shape[1] // nx
    bond_y, width = right.shape
    step = omega.shape[0]
    k, cols, band = ny * step, nx * width, rows // groups
    piece = TILE // chunks
    smem = pl.BlockSpec(memory_space=pltpu.SMEM)
    dma = pltpu.SemaphoreType.DMA
    vmem = pltpu.VMEM

    def sums(first, second):
        return [
            vmem((first, second, per, piece, TILE), F32),
            vmem((2, second // 2, per, piece, TILE), F32),
            vmem((2, second, per, piece, TILE), F32),
            vmem((second, per, piece, TILE), F32),
            vmem((2, per, piece // 2, TILE), F32),
            vmem((2, per, piece, TILE), F32),
        ]

    return pl.pallas_call(
        functools.partial(front_kernel, sizes, per, scale, cross_scale),
        out_shape=(
            jax.ShapeDtypeStruct((band, k), F32),
            jax.ShapeDtypeStruct((ny, nx, nz, nc, per, piece, TILE), F32),
            jax.ShapeDtypeStruct((per, piece, TILE), F32),
            jax.ShapeDtypeStruct((nx, k, width), F32),
        ),
        in_specs=[smem, WHOLE, WHOLE, pl.BlockSpec(memory_space=pl.ANY)],
        out_specs=(WHOLE,) * 4,
        scratch_shapes=[
            vmem((rows, cols), BF16),
            vmem((groups, nx, part, rows), BF16),
            vmem((nx, bond_y * ny, width), BF16),
            vmem((ny, step, cols), BF16),
            vmem((bond_y * ny, rows), BF16),
            vmem((groups, band, k), F32),
            vmem((nz, band, k), F32),
            vmem((2, band // 2, k), F32),
            vmem((2, band, k), F32),
            vmem((groups, band, k), F32),
        ]
        + sums(ny, nx)
        + sums(nx, ny)
        + [dma((nx,)), dma((128,)), dma((128,))],
        compiler_params=pltpu.CompilerParams(vmem_limit_bytes=VMEM_LIMIT, has_side_effects=True),
        name="front",
    )(gate, left, right, omega)


def leaf(rows):
    lane = lax.broadcasted_iota(jnp.int32, (8, HALF), 1)
    sub = lax.broadcasted_iota(jnp.int32, (8, HALF), 0)
    rows = list(rows)
    count = len(rows)
    done = []
    for j in range(count):
        base = 8 * j
        here = (lane >= base) & (lane < base + 8)
        part = rows[j]
        cols = [jnp.broadcast_to(part[:, base + k : base + k + 1], (8, HALF)) for k in range(8)]
        part = jnp.where(here, jnp.where(lane - base == sub, 1.0, 0.0), part)
        tri = jnp.zeros((8, HALF), F32)
        for k in range(8):
            at = sub == k
            pivot = jnp.broadcast_to(cols[k][k : k + 1, :], (8, HALF))
            inv = 1.0 / pivot
            row = jnp.broadcast_to(part[k : k + 1, :], (8, HALF))
            tri = jnp.where(at, row * lax.rsqrt(pivot), tri)
            factor = cols[k] * inv
            part = jnp.where(at, row * inv, part - factor * row)
            for m in range(k + 1, 8):
                mrow = jnp.broadcast_to(cols[m][k : k + 1, :], (8, HALF))
                cols[m] = jnp.where(at, mrow * inv, cols[m] - factor * mrow)
        done.append(jnp.where(lane < base + 8, tri, 0.0))
        if j + 1 < count:
            prow = [jnp.broadcast_to(part[k : k + 1, :], (8, HALF)) for k in range(8)]
            for i in range(j + 1, count):
                mine = rows[i]
                terms = [
                    jnp.broadcast_to(mine[:, base + k : base + k + 1], (8, HALF)) * prow[k]
                    for k in range(8)
                ]
                while len(terms) > 1:
                    terms = [terms[q] + terms[q + 1] for q in range(0, len(terms), 2)]
                rows[i] = jnp.where(here, 0.0, mine) - terms[0]
    return done


def stage_kernel(plan, per, *refs):
    first, stop, nt, chunks, has_carry, has_tiles = plan
    refs = list(refs)
    g_ref = refs.pop(0) if has_tiles else None
    carry_ref = refs.pop(0) if has_carry else None
    uh_ref, ul_ref, inv_ref = refs[:3]
    refs = refs[3:]
    last = stop == nt
    out_ref = None if last else refs.pop(0)
    grid_ref, a_ref, l_ref, uab_ref, sem = refs[:5]
    extra_ref = refs[5] if has_carry and has_tiles else None
    m = (nt - first) * TILE
    size = nt - first
    count = stop - first
    t_ref = grid_ref.reshape(m, m)
    copies = []
    if has_tiles:
        groups = g_ref.shape[0] // chunks
        source = g_ref.reshape(chunks, groups, per, TILE // chunks, TILE)
        target = grid_ref if extra_ref is None else extra_ref
        low, high = (first, stop) if not has_carry else (first, nt)
        for at, (i, j) in enumerate((i, j) for i in range(low, high) for j in range(i, nt)):
            rows = pl.ds((i - first) * chunks, chunks)
            cols = pl.ds((j - first) * TILE, TILE)
            copies.append(
                pltpu.make_async_copy(
                    source.at[:, at // per, at % per], target.at[rows, :, cols], sem.at[0]
                )
            )
    if has_carry:
        for i in range(size):
            at = pl.ds(i * TILE, TILE)
            cols = pl.ds(i * TILE, m - i * TILE)
            copies.append(pltpu.make_async_copy(carry_ref.at[at, cols], t_ref.at[at, cols], sem.at[1]))
    for copy in copies:
        copy.start()
    if not has_carry and not last:
        t_ref[count * TILE :, count * TILE :] = jnp.zeros((m - count * TILE,) * 2, F32)
    for copy in copies:
        copy.wait()
    if extra_ref is not None:
        e_ref = extra_ref.reshape(m, m)

        def add_row(r, carry):
            rat = pl.multiple_of(r * TILE, TILE)

            def add(c, carry):
                cat = pl.multiple_of(c * TILE, TILE)
                t_ref[pl.ds(rat, TILE), pl.ds(cat, TILE)] += e_ref[pl.ds(rat, TILE), pl.ds(cat, TILE)]
                return carry

            return lax.fori_loop(r, size, add, carry)

        lax.fori_loop(0, size, add_row, 0)

    def half(p, h, carry):
        base = pl.multiple_of(p * TILE, TILE)
        mid = pl.multiple_of(p * TILE + HALF, HALF)

        @pl.when(h == 0)
        def _():
            a_ref[...] = t_ref[pl.ds(base, HALF), pl.ds(base, HALF)]

        @pl.when(h == 1)
        def _():
            a_ref[...] = t_ref[pl.ds(mid, HALF), pl.ds(mid, HALF)] - tdot(uab_ref[...], uab_ref[...], HI)

        out = leaf([a_ref[8 * i : 8 * i + 8, :] for i in range(HALF // 8)])
        for i, rows in enumerate(out):
            l_ref[8 * i : 8 * i + 8, :] = rows

        @pl.when(h == 0)
        def _():
            inv_ref[p, 0:HALF, 0:HALF] = l_ref[...]
            inv_ref[p, 0:HALF, HALF:] = jnp.zeros((HALF, HALF), F32)
            uab_ref[...] = jnp.dot(
                l_ref[...], t_ref[pl.ds(base, HALF), pl.ds(mid, HALF)], precision=HI
            )

        @pl.when(h == 1)
        def _():
            cross = tdot(uab_ref[...], inv_ref[p, 0:HALF, 0:HALF], HI)
            inv_ref[p, HALF:, 0:HALF] = -jnp.dot(l_ref[...], cross, precision=HI)
            inv_ref[p, HALF:, HALF:] = l_ref[...]

        return carry

    def panel(p, carry):
        base = pl.multiple_of(p * TILE, TILE)
        lax.fori_loop(0, 2, functools.partial(half, p), 0)

        def row_tile(c, carry):
            at = pl.multiple_of(c * TILE, TILE)
            u = jnp.dot(inv_ref[p], t_ref[pl.ds(base, TILE), pl.ds(at, TILE)], precision=HI)
            head, rest = split(u)
            uh_ref[pl.ds(base, TILE), pl.ds(at, TILE)] = head
            ul_ref[pl.ds(base, TILE), pl.ds(at, TILE)] = rest
            return carry

        lax.fori_loop(p + 1, size, row_tile, 0)

        def trail_row(r, carry):
            rat = pl.multiple_of(r * TILE, TILE)
            head = uh_ref[pl.ds(base, TILE), pl.ds(rat, TILE)].T
            rest = ul_ref[pl.ds(base, TILE), pl.ds(rat, TILE)].T

            def trail(c, carry):
                cat = pl.multiple_of(c * TILE, TILE)
                ch = uh_ref[pl.ds(base, TILE), pl.ds(cat, TILE)]
                cl = ul_ref[pl.ds(base, TILE), pl.ds(cat, TILE)]
                update = jnp.dot(head, ch, preferred_element_type=F32) + (
                    jnp.dot(head, cl, preferred_element_type=F32)
                    + jnp.dot(rest, ch, preferred_element_type=F32)
                )
                t_ref[pl.ds(rat, TILE), pl.ds(cat, TILE)] -= update
                return carry

            lax.fori_loop(r, size, trail, 0)
            return carry

        lax.fori_loop(p + 1, size, trail_row, 0)
        return carry

    lax.fori_loop(0, count, panel, 0)
    if out_ref is not None:
        back = []
        for i in range(count, size):
            at = pl.ds((i - count) * TILE, TILE)
            cols = pl.ds((i - count) * TILE, m - i * TILE)
            mine = t_ref.at[pl.ds(i * TILE, TILE), pl.ds(i * TILE, m - i * TILE)]
            back.append(pltpu.make_async_copy(mine, out_ref.at[at, cols], sem.at[0]))
        for copy in back:
            copy.start()
        for copy in back:
            copy.wait()


def stage(first, stop, n, per, chunks, tiles=None, carry=None):
    nt = n // TILE
    m = n - first * TILE
    rows = (stop - first) * TILE
    piece = TILE // chunks
    args = [v for v in (tiles, carry) if v is not None]
    out_shape = [
        jax.ShapeDtypeStruct((rows, m), BF16),
        jax.ShapeDtypeStruct((rows, m), BF16),
        jax.ShapeDtypeStruct((stop - first, TILE, TILE), F32),
    ]
    out_specs = [WHOLE] * 3
    if stop < nt:
        out_shape.append(jax.ShapeDtypeStruct((m - rows, m - rows), F32))
        out_specs.append(pl.BlockSpec(memory_space=pl.ANY))
    scratch = [
        pltpu.VMEM((m // piece, piece, m), F32),
        pltpu.VMEM((HALF, HALF), F32),
        pltpu.VMEM((HALF, HALF), F32),
        pltpu.VMEM((HALF, HALF), F32),
        pltpu.SemaphoreType.DMA((2,)),
    ]
    if len(args) == 2:
        scratch.append(pltpu.VMEM((m // piece, piece, m), F32))
    plan = (first, stop, nt, chunks, carry is not None, tiles is not None)
    return pl.pallas_call(
        functools.partial(stage_kernel, plan, per),
        out_shape=tuple(out_shape),
        in_specs=[pl.BlockSpec(memory_space=pl.ANY)] * len(args),
        out_specs=tuple(out_specs),
        scratch_shapes=scratch,
        compiler_params=pltpu.CompilerParams(vmem_limit_bytes=VMEM_LIMIT),
        cost_estimate=pl.CostEstimate(
            flops=40 * 10**9, bytes_accessed=rows * m * 8, transcendentals=0
        ),
        name=f"stage{first}",
    )(*args)


def solve_kernel(plan, *refs):
    stages = len(plan)
    factors = refs[: 3 * stages]
    s_ref, w_ref, basis_ref, proj_ref, y_ref = refs[3 * stages : 3 * stages + 5]
    held = refs[3 * stages + 5 : 6 * stages + 5]
    sem = refs[6 * stages + 5]
    copies = [
        pltpu.make_async_copy(a, b, sem.at[q]) for q, (a, b) in enumerate(zip(factors, held))
    ]
    for copy in copies:
        copy.start()
    mine, n = s_ref.shape
    nt = n // TILE
    padded = jnp.concatenate([s_ref[...], jnp.zeros((HALF - mine, n), F32)], axis=0)
    y_ref[:, :HALF] = padded.T
    y_ref[:, HALF:] = w_ref[...]
    for q, (first, stop) in enumerate(plan):
        uh_ref, ul_ref, inv_ref = held[3 * q : 3 * q + 3]
        for copy in copies[3 * q : 3 * q + 3]:
            copy.wait()
        for p in range(first, stop):
            rows = slice(p * TILE, (p + 1) * TILE)
            local = slice((p - first) * TILE, (p - first + 1) * TILE)
            y = jnp.dot(inv_ref[p - first], y_ref[rows, :], precision=HI)
            y_ref[rows, :] = y
            proj_ref[rows, :] = y[:, HALF:]
            head, rest = split(y)

            def tail(r, carry):
                at = pl.multiple_of(r * TILE, TILE)
                here = pl.multiple_of((r - first) * TILE, TILE)
                uh = uh_ref[local, pl.ds(here, TILE)]
                ul = ul_ref[local, pl.ds(here, TILE)]
                y_ref[pl.ds(at, TILE), :] -= tdot(uh, head) + (tdot(uh, rest) + tdot(ul, head))
                return carry

            lax.fori_loop(p + 1, nt, tail, 0)
    basis_ref[...] = y_ref[:, :HALF].T[:mine]


def solve(plan, factors, sketch, weights):
    mine, n = sketch.shape
    flat = [v for part in factors for v in part]
    return pl.pallas_call(
        functools.partial(solve_kernel, plan),
        out_shape=(jax.ShapeDtypeStruct((mine, n), F32), jax.ShapeDtypeStruct((n, HALF), F32)),
        in_specs=[pl.BlockSpec(memory_space=pl.ANY)] * len(flat) + [WHOLE, WHOLE],
        out_specs=(WHOLE, WHOLE),
        scratch_shapes=[pltpu.VMEM((n, 2 * HALF), F32)]
        + [pltpu.VMEM(v.shape, v.dtype) for v in flat]
        + [pltpu.SemaphoreType.DMA((len(flat),))],
        compiler_params=pltpu.CompilerParams(vmem_limit_bytes=VMEM_LIMIT),
        name="solve",
    )(*flat, sketch, weights)


CUTS = ((0, 3), (3, 6), (6, 9))


def tile_halves(nt):
    cut = CUTS[0][1]
    return (0, cut), (cut, nt)


def tiles_each(nt, groups):
    counts = [sum(nt - i for i in range(low, high)) for low, high in tile_halves(nt)]
    return -(-max(counts) // groups)


def on_device(left_site, right_site, gate, omega):
    sizes = tuple(lax.axis_size(a) for a in ("row", "x", "z", "core"))
    ny, nx, nz, nc = sizes
    total = left_site.shape[0] * ny
    width = right_site.shape[1]
    n = omega.shape[1] * ny
    chunks = ny * nx
    per = tiles_each(n // TILE, nz * nc)
    sketch, early, late, weights = front(
        gate, left_site.T, right_site, omega.T, sizes, per, 1.0 / total, 1.0 / math_sqrt(total)
    )
    early = early.reshape((ny * nx * nz * nc,) + early.shape[4:])
    late = lax.all_gather(late[None], ("row", "x", "z", "core"), axis=0, tiled=True)

    *part_a, carry = stage(*CUTS[0], n, per, chunks, tiles=early)
    carry, weights = lax.optimization_barrier((carry, weights))
    weights = lax.psum_scatter(weights, "x", scatter_dimension=0, tiled=True)
    *part_b, carry = stage(*CUTS[1], n, per, chunks, tiles=late, carry=carry)
    carry, weights = lax.optimization_barrier((carry, weights))
    weights = lax.psum(weights, "row").reshape(n, width)
    part_c = stage(*CUTS[2], n, per, chunks, carry=carry)
    basis, projected = solve(CUTS, (part_a, part_b, part_c), sketch, weights)
    block = n // ny
    return basis, lax.dynamic_slice_in_dim(projected, lax.axis_index("row") * block, block, 0)


def math_sqrt(value):
    return float(np.sqrt(value))


def solution(mesh):
    fine = Mesh(mesh.devices.reshape(4, 4, 4, 2), ("row", "x", "z", "core"))
    col = ("x", "z", "core")
    in_specs = (P("row", col), P("row", col), P(), P(None, "row"))
    out_specs = (P(("row",) + col, None), P("row", col))
    return jax.shard_map(on_device, mesh=fine, in_specs=in_specs, out_specs=out_specs, check_vma=False)
```

```python
import functools

import jax
import jax.numpy as jnp
import numpy as np
from jax import lax
from jax.experimental import pallas as pl
from jax.experimental.pallas import tpu as pltpu
from jax.sharding import Mesh
from jax.sharding import PartitionSpec as P

HI = lax.Precision.HIGHEST
F32, BF16 = jnp.float32, jnp.bfloat16
TILE = 256
HALF = 128
TASKS = 7
VMEM_LIMIT = 60 << 20
WHOLE = pl.BlockSpec(memory_space=pltpu.VMEM)


def split(x):
    head = x.astype(BF16)
    return head, (x - head.astype(F32)).astype(BF16)


def tdot(a, b, precision=None):
    return lax.dot_general(
        a, b, (((0,), (0,)), ((), ())), preferred_element_type=F32, precision=precision
    )


def near(index, size, step):
    return lax.rem(index + (step + size), size)


def front_kernel(
    sizes, per, scale, cross_scale, gate_ref, left_ref, right_ref, omega_hbm,
    mine_ref, early_ref, late_ref, cross_ref,
    theta_ref, all_left, all_right, all_omega, bond_ref,
    part_ref, pair_ref, relay_ref, got_ref, held_ref,
    ya_ref, ya_relay, ya_got, xa_ref, xa_relay, xa_got,
    xb_ref, xb_relay, xb_got, yb_ref, yb_relay, yb_got,
    local, send, recv,
):
    ny, nx, nz, nc = sizes
    groups = nz * nc
    y, x, z, c = (lax.axis_index(a) for a in ("row", "x", "z", "core"))
    zc = z * nc + c
    twin = (y, x, z, 1 - c)
    part = left_ref.shape[0]
    rows = all_left.shape[3]
    bond_y, width = right_ref.shape
    step = omega_hbm.shape[0]
    band = rows // groups
    moves = []

    def push(src, dst, to):
        at = len(moves)
        move = pltpu.make_async_remote_copy(
            src_ref=src, dst_ref=dst, send_sem=send.at[at], recv_sem=recv.at[at],
            device_id=to, device_id_type=pl.DeviceIdType.MESH,
        )
        moves.append(move)
        return move

    def beside(axis, way):
        place = [y, x, z, c]
        place[axis] = near(place[axis], sizes[axis], way)
        return tuple(place)

    class Gather:
        def __init__(self, axis, block):
            me = (y, x, z)[axis]
            self.below, self.above = near(me, 4, -1), near(me, 4, 1)
            up, down = beside(axis, 1), beside(axis, -1)
            own = block(me, None)
            self.up, self.down = push(own, own, up), push(own, own, down)
            first, second = block(self.below, 0), block(self.above, 1)
            self.far_up, self.far_down = push(first, first, up), push(second, second, down)

        def start(self):
            self.up.start()
            self.down.start()

        def relay(self):
            self.up.wait_recv()
            self.far_up.start()
            self.down.wait_recv()
            self.far_down.start()

        def finish(self):
            self.far_up.wait_recv()
            self.far_down.wait_recv()

    class Reduce:
        def __init__(self, axis, block, relay, got):
            me = (y, x, z)[axis]
            up, down = beside(axis, 1), beside(axis, -1)
            far, above, below = near(me, 4, 2), near(me, 4, 1), near(me, 4, -1)
            self.block, self.me, self.above, self.below, self.far = block, me, above, below, far
            self.relay, self.got = relay, got
            self.far_up = push(block(far, 0), relay.at[0], up)
            self.far_down = push(block(far, 1), relay.at[1], down)
            self.up = push(block(above, None), got.at[0], up)
            self.down = push(block(below, None), got.at[1], down)

        def start(self):
            self.far_up.start()
            self.far_down.start()

        def middle(self):
            self.far_up.wait_recv()
            self.block(self.above, 0)[...] += self.relay[0]
            self.up.start()
            self.far_down.wait_recv()
            self.block(self.below, 1)[...] += self.relay[1]
            self.down.start()

        def finish(self):
            self.up.wait_recv()
            self.down.wait_recv()
            return self.block(self.me, None)[...] + self.got[0] + self.got[1]

    def halved(ref, rows_of, half):
        return ref if half is None else ref.at[pl.ds(half * (rows_of // 2), rows_of // 2)]

    def right_y(slot, half):
        size = bond_y if half is None else bond_y // 2
        begin = slot * bond_y + (0 if half is None else half * size)
        return all_right.at[x, pl.ds(pl.multiple_of(begin, 128), size), :]

    own_omega = [
        pltpu.make_async_copy(
            omega_hbm.at[:, pl.ds(pl.multiple_of((q * groups + zc) * width, width), width)],
            all_omega.at[y, :, pl.ds(q * width, width)], local.at[q],
        )
        for q in range(nx)
    ]
    for move in own_omega:
        move.start()
    all_right[x, pl.ds(pl.multiple_of(y * bond_y, bond_y), bond_y), :] = right_ref[...]
    by_y = Gather(0, right_y)
    by_y.start()
    across = []
    for dx in range(1, nx):
        to_x = near(x, nx, dx)
        src = left_ref.at[:, pl.ds(pl.multiple_of(to_x * rows, rows), rows)]
        across.append(push(src, all_left.at[zc, x], (y, to_x, z, c)))
    for move in across:
        move.start()
    all_left[zc, x] = left_ref[:, pl.ds(pl.multiple_of(x * rows, rows), rows)]

    def right_x(row):
        at = pl.ds(pl.multiple_of(row * bond_y, bond_y), bond_y)

        def block(slot, half):
            if half is None:
                return all_right.at[slot, at, :]
            size = bond_y // 2
            return all_right.at[slot, pl.ds(pl.multiple_of(row * bond_y + half * size, size), size), :]

        return Gather(1, block)

    by_x = [right_x(near(y, ny, d)) for d in (0, -1, 1, 2)]
    by_x[0].start()
    by_y.up.wait_recv()
    by_y.far_up.start()
    by_x[1].start()
    by_y.down.wait_recv()
    by_y.far_down.start()
    by_x[2].start()
    for move in own_omega:
        move.wait()
    omega_y = Gather(0, lambda slot, half: halved(all_omega.at[slot], step, half))
    omega_y.start()
    for move in across:
        move.wait_recv()
    left_z = Gather(2, lambda slot, half: halved(all_left.at[slot * nc + c], nx, half))
    left_z.start()
    left_twin = [push(all_left.at[near(z, nz, d) * nc + c], all_left.at[near(z, nz, d) * nc + c], twin)
                 for d in (0, -1, 1, 2)]
    left_twin[0].start()
    by_x[0].relay()
    by_y.finish()
    by_x[3].start()
    left_z.relay()
    left_twin[1].start()
    left_twin[2].start()
    by_x[1].relay()
    by_x[2].relay()
    left_z.finish()
    left_twin[3].start()
    by_x[3].relay()
    omega_y.relay()
    for move in left_twin:
        move.wait_recv()
    for xs in range(nx):
        for g in range(groups):
            at = (xs * groups + g) * part
            bond_ref[at : at + part, :] = all_left[g, xs]
    for ring in by_x:
        ring.finish()

    left = bond_ref[...]
    row_odd = lax.broadcasted_iota(jnp.int32, (rows, width), 0) % 2 == 1
    col_odd = lax.broadcasted_iota(jnp.int32, (rows, width), 1) % 2 == 1

    def coupling(row_flip, col_flip):
        def entry(s1, s2):
            a, b = s1 ^ row_flip, s2 ^ col_flip
            return gate_ref[2 * s1 + s2, 2 * a + b]

        even = jnp.where(col_odd, entry(0, 1), entry(0, 0))
        odd = jnp.where(col_odd, entry(1, 1), entry(1, 0))
        return jnp.where(row_odd, odd, even)

    for xs in range(nx):
        bare = tdot(left, all_right[xs])
        row_partner = jnp.where(row_odd, pltpu.roll(bare, 1, 0), pltpu.roll(bare, rows - 1, 0))

        def col_partner(v):
            return jnp.where(col_odd, pltpu.roll(v, 1, 1), pltpu.roll(v, width - 1, 1))

        mixed = (coupling(0, 0) * bare + coupling(0, 1) * col_partner(bare)) + (
            coupling(1, 0) * row_partner + coupling(1, 1) * col_partner(row_partner)
        )
        theta_ref[:, xs * width : (xs + 1) * width] = mixed.astype(BF16)
    omega_y.finish()
    theta = theta_ref[...]
    for q in range(ny):
        value = lax.dot_general(
            theta, all_omega[q], (((1,), (1,)), ((), ())), preferred_element_type=F32
        )
        part_ref[:, :, q * step : (q + 1) * step] = value.reshape(groups, band, step)

    order = (2, 1, -1, 0)
    pairs = [
        push(part_ref.at[near(z, nz, d) * nc + 1 - c], pair_ref.at[q], twin) for q, d in enumerate(order)
    ]
    for move in pairs:
        move.start()

    def block_z(slot, half):
        return halved(part_ref.at[slot * nc + c], band, half)

    def add_pair(q):
        pairs[q].wait_recv()
        part_ref[near(z, nz, order[q]) * nc + c] += pair_ref[q]

    sum_z = Reduce(2, block_z, relay_ref, got_ref)
    add_pair(0)
    sum_z.start()
    add_pair(1)
    add_pair(2)
    sum_z.middle()
    add_pair(3)
    total = sum_z.finish()
    held_ref[zc] = total

    rows_z = Gather(2, lambda slot, half: halved(held_ref.at[slot * nc + c], band, half))
    rows_z.start()
    rows_twin = [push(held_ref.at[near(z, nz, d) * nc + c], held_ref.at[near(z, nz, d) * nc + c], twin)
                 for d in (0, -1, 1, 2)]
    rows_twin[0].start()
    mine_ref[...] = total
    rows_z.relay()
    rows_twin[1].start()
    rows_twin[2].start()
    rows_z.finish()
    rows_twin[3].start()
    for move in rows_twin:
        move.wait_recv()
    k = mine_ref.shape[1]
    nt = k // TILE
    piece = early_ref.shape[5]

    def columns(at, count=TILE):
        return held_ref[:, :, pl.ds(at, count)].reshape(rows, count)

    def tiles(half, out):
        low, high = tile_halves(nt)[half]
        starts = [0]
        for i in range(low, high):
            starts.append(starts[-1] + nt - i)

        def tile(t, carry):
            at = jnp.minimum(zc * per + t, starts[-1] - 1)
            row, begin = jnp.int32(low), jnp.int32(0)
            for q in range(1, len(starts) - 1):
                row = jnp.where(at >= starts[q], low + q, row)
                begin = jnp.where(at >= starts[q], starts[q], begin)
            i = pl.multiple_of(row * TILE, TILE)
            j = pl.multiple_of((row + at - begin) * TILE, TILE)
            value = tdot(columns(i), columns(j), HI) * scale
            for q in range(ny):
                for r in range(nx):
                    at = (q * nx + r) * piece
                    spot = (q, r) if half == 0 else (r, q)
                    out[spot[0], spot[1], pl.ds(t, 1)] = value[at : at + piece].reshape(1, piece, TILE)
            return carry

        lax.fori_loop(0, per, tile, 0)

    def lower_rows(ref, slot, half):
        if half is None:
            return ref.at[slot]
        return ref.at[slot, :, pl.ds(half * (piece // 2), piece // 2)]

    first_a = Reduce(0, lambda s, h: halved(ya_ref.at[s], nx, h), ya_relay, ya_got)
    first_b = Reduce(1, lambda s, h: halved(xb_ref.at[s], ny, h), xb_relay, xb_got)
    tiles(0, ya_ref)
    first_a.start()
    tiles(1, xb_ref)
    first_a.middle()
    first_b.start()
    xa_ref[...] = first_a.finish()
    then_a = Reduce(1, lambda s, h: lower_rows(xa_ref, s, h), xa_relay, xa_got)
    then_a.start()
    first_b.middle()
    then_a.middle()
    yb_ref[...] = first_b.finish()
    then_b = Reduce(0, lambda s, h: lower_rows(yb_ref, s, h), yb_relay, yb_got)
    then_b.start()
    early_ref[y, x, z, c] = then_a.finish()

    spots = ((2, 0, 1), (0, 1, 2), (1, 2, 0))
    here = (y, x, z)

    def plane(t, phase):
        axes = spots[t]
        along = axes[phase]

        def block(slot, half):
            index = [here[0], here[1], here[2]]
            for done in axes[:phase]:
                index[done] = slice(None)
            index[along] = slot
            if half is not None and phase == 0:
                rows_at = pl.ds(half * (piece // 2), piece // 2)
                return early_ref.at[index[0], index[1], index[2], c, t, rows_at]
            if half is not None:
                index[axes[0]] = pl.ds(2 * half, 2)
            return early_ref.at[index[0], index[1], index[2], c, t]

        return along, block

    rings = []
    for t in range(per):
        along, block = plane(t, 0)
        rings.append(Gather(along, block))
        rings[t].start()
    then_b.middle()
    for ring in rings:
        ring.relay()
    late_ref[...] = then_b.finish()
    second = []
    for t in range(per):
        rings[t].finish()
        along, block = plane(t, 1)
        second.append(Gather(along, block))
        second[t].start()
    for ring in second:
        ring.relay()
    third, to_twin = [], []
    for t in range(per):
        second[t].finish()
        along, block = plane(t, 2)
        third.append(Gather(along, block))
        third[t].start()
        me = here[along]
        group = []
        for d in (0, -1, 1, 2):
            ref = block(near(me, 4, d), None)
            group.append(push(ref, ref, twin))
        to_twin.append(group)
        group[0].start()

    theta = theta_ref[...]
    for at in range(0, k, TILE):
        head, rest = split(columns(at))
        value = (tdot(head, theta) + tdot(rest, theta)) * cross_scale
        for q in range(nx):
            cross_ref[q, at : at + TILE, :] = value[:, q * width : (q + 1) * width]

    for t in range(per):
        third[t].relay()
        to_twin[t][1].start()
        to_twin[t][2].start()
    for t in range(per):
        third[t].finish()
        to_twin[t][3].start()
    for group in to_twin:
        for move in group:
            move.wait_recv()
    for move in moves:
        move.wait_send()


def front(gate, left, right, omega, sizes, per, scale, cross_scale):
    ny, nx, nz, nc = sizes
    groups, chunks = nz * nc, ny * nx
    part, rows = left.shape[0], left.shape[1] // nx
    bond_y, width = right.shape
    step = omega.shape[0]
    k, cols, band = ny * step, nx * width, rows // groups
    piece = TILE // chunks
    smem = pl.BlockSpec(memory_space=pltpu.SMEM)
    dma = pltpu.SemaphoreType.DMA
    vmem = pltpu.VMEM

    def sums(first, second):
        return [
            vmem((first, second, per, piece, TILE), F32),
            vmem((2, second // 2, per, piece, TILE), F32),
            vmem((2, second, per, piece, TILE), F32),
            vmem((second, per, piece, TILE), F32),
            vmem((2, per, piece // 2, TILE), F32),
            vmem((2, per, piece, TILE), F32),
        ]

    return pl.pallas_call(
        functools.partial(front_kernel, sizes, per, scale, cross_scale),
        out_shape=(
            jax.ShapeDtypeStruct((band, k), F32),
            jax.ShapeDtypeStruct((ny, nx, nz, nc, per, piece, TILE), F32),
            jax.ShapeDtypeStruct((per, piece, TILE), F32),
            jax.ShapeDtypeStruct((nx, k, width), F32),
        ),
        in_specs=[smem, WHOLE, WHOLE, pl.BlockSpec(memory_space=pl.ANY)],
        out_specs=(WHOLE,) * 4,
        scratch_shapes=[
            vmem((rows, cols), BF16),
            vmem((groups, nx, part, rows), BF16),
            vmem((nx, bond_y * ny, width), BF16),
            vmem((ny, step, cols), BF16),
            vmem((bond_y * ny, rows), BF16),
            vmem((groups, band, k), F32),
            vmem((nz, band, k), F32),
            vmem((2, band // 2, k), F32),
            vmem((2, band, k), F32),
            vmem((groups, band, k), F32),
        ]
        + sums(ny, nx)
        + sums(nx, ny)
        + [dma((nx,)), dma((128,)), dma((128,))],
        compiler_params=pltpu.CompilerParams(vmem_limit_bytes=VMEM_LIMIT, has_side_effects=True),
        name="front",
    )(gate, left, right, omega)


def leaf(rows, task=None, tasks=0):
    lane = lax.broadcasted_iota(jnp.int32, (8, HALF), 1)
    sub = lax.broadcasted_iota(jnp.int32, (8, HALF), 0)
    rows = list(rows)
    count = len(rows)
    done = []
    for j in range(count):
        base = 8 * j
        here = (lane >= base) & (lane < base + 8)
        part = rows[j]
        cols = [jnp.broadcast_to(part[:, base + k : base + k + 1], (8, HALF)) for k in range(8)]
        part = jnp.where(here, jnp.where(lane - base == sub, 1.0, 0.0), part)
        tri = jnp.zeros((8, HALF), F32)
        for k in range(8):
            at = sub == k
            pivot = jnp.broadcast_to(cols[k][k : k + 1, :], (8, HALF))
            inv = 1.0 / pivot
            row = jnp.broadcast_to(part[k : k + 1, :], (8, HALF))
            tri = jnp.where(at, row * lax.rsqrt(pivot), tri)
            factor = cols[k] * inv
            part = jnp.where(at, row * inv, part - factor * row)
            for m in range(k + 1, 8):
                mrow = jnp.broadcast_to(cols[m][k : k + 1, :], (8, HALF))
                cols[m] = jnp.where(at, mrow * inv, cols[m] - factor * mrow)
        done.append(jnp.where(lane < base + 8, tri, 0.0))
        for extra in range(j * tasks // count, (j + 1) * tasks // count):
            task(extra)
        if j + 1 < count:
            prow = [jnp.broadcast_to(part[k : k + 1, :], (8, HALF)) for k in range(8)]
            for i in range(j + 1, count):
                mine = rows[i]
                terms = [
                    jnp.broadcast_to(mine[:, base + k : base + k + 1], (8, HALF)) * prow[k]
                    for k in range(8)
                ]
                while len(terms) > 1:
                    terms = [terms[q] + terms[q + 1] for q in range(0, len(terms), 2)]
                rows[i] = jnp.where(here, 0.0, mine) - terms[0]
    return done


def stage_kernel(plan, per, *refs):
    first, stop, nt, chunks, has_carry, has_tiles = plan
    refs = list(refs)
    g_ref = refs.pop(0) if has_tiles else None
    carry_ref = refs.pop(0) if has_carry else None
    uh_ref, ul_ref, inv_ref = refs[:3]
    refs = refs[3:]
    last = stop == nt
    out_ref = None if last else refs.pop(0)
    grid_ref, a_ref, l_ref, uab_ref, s3_ref, t3_ref, sem = refs[:7]
    extra_ref = refs[7] if has_carry and has_tiles else None
    m = (nt - first) * TILE
    size = nt - first
    count = stop - first
    t_ref = grid_ref.reshape(m, m)
    copies = []
    if has_tiles:
        groups = g_ref.shape[0] // chunks
        source = g_ref.reshape(chunks, groups, per, TILE // chunks, TILE)
        target = grid_ref if extra_ref is None else extra_ref
        low, high = (first, stop) if not has_carry else (first, nt)
        for at, (i, j) in enumerate((i, j) for i in range(low, high) for j in range(i, nt)):
            rows = pl.ds((i - first) * chunks, chunks)
            cols = pl.ds((j - first) * TILE, TILE)
            copies.append(
                pltpu.make_async_copy(
                    source.at[:, at // per, at % per], target.at[rows, :, cols], sem.at[0]
                )
            )
    if has_carry:
        for i in range(size):
            at = pl.ds(i * TILE, TILE)
            cols = pl.ds(i * TILE, m - i * TILE)
            copies.append(pltpu.make_async_copy(carry_ref.at[at, cols], t_ref.at[at, cols], sem.at[1]))
    for copy in copies:
        copy.start()
    if not has_carry and not last:
        t_ref[count * TILE :, count * TILE :] = jnp.zeros((m - count * TILE,) * 2, F32)
    for copy in copies:
        copy.wait()
    if extra_ref is not None:
        e_ref = extra_ref.reshape(m, m)

        def add_row(r, carry):
            rat = pl.multiple_of(r * TILE, TILE)

            def add(c, carry):
                cat = pl.multiple_of(c * TILE, TILE)
                t_ref[pl.ds(rat, TILE), pl.ds(cat, TILE)] += e_ref[pl.ds(rat, TILE), pl.ds(cat, TILE)]
                return carry

            return lax.fori_loop(r, size, add, carry)

        lax.fori_loop(0, size, add_row, 0)

    def in_row(r):
        return (size - r + 1) // 2

    def total_tasks(p):
        left = size - 1 - p
        pairs = left // 2
        count = jnp.where(left % 2 == 0, pairs * (pairs + 1), (pairs + 1) * (pairs + 1)) - 1
        return jnp.where((p < 0) | (left < 1), 0, count)

    def apply(r, q):
        rat = pl.multiple_of(r * TILE, TILE)
        cat = pl.multiple_of((size - 2 - 2 * q) * TILE, TILE)
        t_ref[pl.ds(rat, TILE), pl.ds(cat, 2 * TILE)] -= jnp.dot(
            t3_ref[pl.ds(rat, TILE), :], s3_ref[:, pl.ds(cat, 2 * TILE)], preferred_element_type=F32
        )

    def update(p, at):
        row, begin, start = p + 1, jnp.int32(0), in_row(p + 1) - 1
        for _ in range(size - 2):
            nxt = at >= start
            begin = jnp.where(nxt, start, begin)
            row = jnp.where(nxt, row + 1, row)
            start = jnp.where(nxt, start + in_row(row), start)
        apply(row, at - begin)

    def half(p, h, carry):
        base = pl.multiple_of(p * TILE, TILE)
        mid = pl.multiple_of(p * TILE + HALF, HALF)

        @pl.when(h == 0)
        def _():
            a_ref[...] = t_ref[pl.ds(base, HALF), pl.ds(base, HALF)]

        @pl.when(h == 1)
        def _():
            a_ref[...] = t_ref[pl.ds(mid, HALF), pl.ds(mid, HALF)] - tdot(uab_ref[...], uab_ref[...], HI)

        done = carry
        busy = done + TASKS <= total_tasks(p - 1) if size > 4 else False

        def factor(task=None, tasks=0):
            out = leaf([a_ref[8 * i : 8 * i + 8, :] for i in range(HALF // 8)], task, tasks)
            for i, rows in enumerate(out):
                l_ref[8 * i : 8 * i + 8, :] = rows

        if size > 4:

            @pl.when(busy)
            def _():
                factor(lambda extra: update(p - 1, done + extra), TASKS)

            @pl.when(jnp.logical_not(busy))
            def _():
                factor()

        else:
            factor()

        @pl.when(h == 0)
        def _():
            inv_ref[p, 0:HALF, 0:HALF] = l_ref[...]
            inv_ref[p, 0:HALF, HALF:] = jnp.zeros((HALF, HALF), F32)
            uab_ref[...] = jnp.dot(
                l_ref[...], t_ref[pl.ds(base, HALF), pl.ds(mid, HALF)], precision=HI
            )

        @pl.when(h == 1)
        def _():
            cross = tdot(uab_ref[...], inv_ref[p, 0:HALF, 0:HALF], HI)
            inv_ref[p, HALF:, 0:HALF] = -jnp.dot(l_ref[...], cross, precision=HI)
            inv_ref[p, HALF:, HALF:] = l_ref[...]

        return jnp.where(busy, done + TASKS, done)

    def panel(p, carry):
        base = pl.multiple_of(p * TILE, TILE)
        done = lax.fori_loop(0, 2, functools.partial(half, p), jnp.int32(0))

        def rest(at, carry):
            update(p - 1, at)
            return carry

        lax.fori_loop(done, total_tasks(p - 1), rest, 0)

        def row_tile(c, carry):
            at = pl.multiple_of(c * TILE, TILE)
            u = jnp.dot(inv_ref[p], t_ref[pl.ds(base, TILE), pl.ds(at, TILE)], precision=HI)
            head, rest = split(u)
            uh_ref[pl.ds(base, TILE), pl.ds(at, TILE)] = head
            ul_ref[pl.ds(base, TILE), pl.ds(at, TILE)] = rest
            for third, value in enumerate((head, rest, head)):
                s3_ref[third * TILE : (third + 1) * TILE, pl.ds(at, TILE)] = value
            for third, value in enumerate((head.T, head.T, rest.T)):
                t3_ref[pl.ds(at, TILE), third * TILE : (third + 1) * TILE] = value
            return carry

        lax.fori_loop(p + 1, size, row_tile, 0)

        @pl.when(p + 1 < size)
        def _():
            apply(p + 1, in_row(p + 1) - 1)

        return carry

    lax.fori_loop(0, count, panel, 0)
    if not last:

        def rest(at, carry):
            update(count - 1, at)
            return carry

        lax.fori_loop(0, total_tasks(count - 1), rest, 0)
    if out_ref is not None:
        back = []
        for i in range(count, size):
            at = pl.ds((i - count) * TILE, TILE)
            cols = pl.ds((i - count) * TILE, m - i * TILE)
            mine = t_ref.at[pl.ds(i * TILE, TILE), pl.ds(i * TILE, m - i * TILE)]
            back.append(pltpu.make_async_copy(mine, out_ref.at[at, cols], sem.at[0]))
        for copy in back:
            copy.start()
        for copy in back:
            copy.wait()


def stage(first, stop, n, per, chunks, tiles=None, carry=None):
    nt = n // TILE
    m = n - first * TILE
    rows = (stop - first) * TILE
    piece = TILE // chunks
    args = [v for v in (tiles, carry) if v is not None]
    out_shape = [
        jax.ShapeDtypeStruct((rows, m), BF16),
        jax.ShapeDtypeStruct((rows, m), BF16),
        jax.ShapeDtypeStruct((stop - first, TILE, TILE), F32),
    ]
    out_specs = [WHOLE] * 3
    if stop < nt:
        out_shape.append(jax.ShapeDtypeStruct((m - rows, m - rows), F32))
        out_specs.append(pl.BlockSpec(memory_space=pl.ANY))
    scratch = [
        pltpu.VMEM((m // piece, piece, m), F32),
        pltpu.VMEM((HALF, HALF), F32),
        pltpu.VMEM((HALF, HALF), F32),
        pltpu.VMEM((HALF, HALF), F32),
        pltpu.VMEM((3 * TILE, m), BF16),
        pltpu.VMEM((m, 3 * TILE), BF16),
        pltpu.SemaphoreType.DMA((2,)),
    ]
    if len(args) == 2:
        scratch.append(pltpu.VMEM((m // piece, piece, m), F32))
    plan = (first, stop, nt, chunks, carry is not None, tiles is not None)
    return pl.pallas_call(
        functools.partial(stage_kernel, plan, per),
        out_shape=tuple(out_shape),
        in_specs=[pl.BlockSpec(memory_space=pl.ANY)] * len(args),
        out_specs=tuple(out_specs),
        scratch_shapes=scratch,
        compiler_params=pltpu.CompilerParams(vmem_limit_bytes=VMEM_LIMIT),
        cost_estimate=pl.CostEstimate(
            flops=40 * 10**9, bytes_accessed=rows * m * 8, transcendentals=0
        ),
    )(*args)


def solve_kernel(plan, *refs):
    stages = len(plan)
    factors = refs[: 3 * stages]
    s_ref, w_ref, basis_ref, proj_ref, y_ref = refs[3 * stages : 3 * stages + 5]
    held = refs[3 * stages + 5 : 6 * stages + 5]
    sem = refs[6 * stages + 5]
    copies = [
        pltpu.make_async_copy(a, b, sem.at[q]) for q, (a, b) in enumerate(zip(factors, held))
    ]
    for copy in copies:
        copy.start()
    mine, n = s_ref.shape
    nt = n // TILE
    padded = jnp.concatenate([s_ref[...], jnp.zeros((HALF - mine, n), F32)], axis=0)
    y_ref[:, :HALF] = padded.T
    y_ref[:, HALF:] = w_ref[...]
    for q, (first, stop) in enumerate(plan):
        uh_ref, ul_ref, inv_ref = held[3 * q : 3 * q + 3]
        for copy in copies[3 * q : 3 * q + 3]:
            copy.wait()
        for p in range(first, stop):
            rows = slice(p * TILE, (p + 1) * TILE)
            local = slice((p - first) * TILE, (p - first + 1) * TILE)
            y = jnp.dot(inv_ref[p - first], y_ref[rows, :], precision=HI)
            y_ref[rows, :] = y
            proj_ref[rows, :] = y[:, HALF:]
            head, rest = split(y)

            def tail(r, carry):
                at = pl.multiple_of(r * TILE, TILE)
                here = pl.multiple_of((r - first) * TILE, TILE)
                uh = uh_ref[local, pl.ds(here, TILE)]
                ul = ul_ref[local, pl.ds(here, TILE)]
                y_ref[pl.ds(at, TILE), :] -= tdot(uh, head) + (tdot(uh, rest) + tdot(ul, head))
                return carry

            lax.fori_loop(p + 1, nt, tail, 0)
    basis_ref[...] = y_ref[:, :HALF].T[:mine]


def solve(plan, factors, sketch, weights):
    mine, n = sketch.shape
    flat = [v for part in factors for v in part]
    return pl.pallas_call(
        functools.partial(solve_kernel, plan),
        out_shape=(jax.ShapeDtypeStruct((mine, n), F32), jax.ShapeDtypeStruct((n, HALF), F32)),
        in_specs=[pl.BlockSpec(memory_space=pl.ANY)] * len(flat) + [WHOLE, WHOLE],
        out_specs=(WHOLE, WHOLE),
        scratch_shapes=[pltpu.VMEM((n, 2 * HALF), F32)]
        + [pltpu.VMEM(v.shape, v.dtype) for v in flat]
        + [pltpu.SemaphoreType.DMA((len(flat),))],
        compiler_params=pltpu.CompilerParams(vmem_limit_bytes=VMEM_LIMIT),
        name="solve",
    )(*flat, sketch, weights)


CUTS = ((0, 3), (3, 6), (6, 9))


def tile_halves(nt):
    cut = CUTS[0][1]
    return (0, cut), (cut, nt)


def tiles_each(nt, groups):
    counts = [sum(nt - i for i in range(low, high)) for low, high in tile_halves(nt)]
    return -(-max(counts) // groups)


def on_device(left_site, right_site, gate, omega):
    sizes = tuple(lax.axis_size(a) for a in ("row", "x", "z", "core"))
    ny, nx, nz, nc = sizes
    total = left_site.shape[0] * ny
    width = right_site.shape[1]
    n = omega.shape[1] * ny
    chunks = ny * nx
    per = tiles_each(n // TILE, nz * nc)
    sketch, early, late, weights = front(
        gate, left_site.T, right_site, omega.T, sizes, per, 1.0 / total, 1.0 / math_sqrt(total)
    )
    early = early.reshape((ny * nx * nz * nc,) + early.shape[4:])
    late = lax.all_gather(late[None], ("row", "x", "z", "core"), axis=0, tiled=True)
    weights = lax.psum_scatter(weights, "x", scatter_dimension=0, tiled=True)

    *part_a, carry = stage(*CUTS[0], n, per, chunks, tiles=early)
    *part_b, carry = stage(*CUTS[1], n, per, chunks, tiles=late, carry=carry)
    carry, weights = lax.optimization_barrier((carry, weights))
    weights = lax.psum(weights, "row").reshape(n, width)
    part_c = stage(*CUTS[2], n, per, chunks, carry=carry)
    basis, projected = solve(CUTS, (part_a, part_b, part_c), sketch, weights)
    block = n // ny
    return basis, lax.dynamic_slice_in_dim(projected, lax.axis_index("row") * block, block, 0)


def math_sqrt(value):
    return float(np.sqrt(value))


def solution(mesh):
    fine = Mesh(mesh.devices.reshape(4, 4, 4, 2), ("row", "x", "z", "core"))
    col = ("x", "z", "core")
    in_specs = (P("row", col), P("row", col), P(), P(None, "row"))
    out_specs = (P(("row",) + col, None), P("row", col))
    return jax.shard_map(
        on_device, mesh=fine, in_specs=in_specs, out_specs=out_specs, check_vma=False
    )
```

```python
import functools

import jax
import jax.numpy as jnp
import numpy as np
from jax import lax
from jax.experimental import pallas as pl
from jax.experimental.pallas import tpu as pltpu
from jax.sharding import Mesh
from jax.sharding import PartitionSpec as P

HI = lax.Precision.HIGHEST
F32, BF16 = jnp.float32, jnp.bfloat16
TILE = 256
HALF = 128
TASKS = 7
VMEM_LIMIT = 60 << 20
WHOLE = pl.BlockSpec(memory_space=pltpu.VMEM)


def split(x):
    head = x.astype(BF16)
    return head, (x - head.astype(F32)).astype(BF16)


def tdot(a, b, precision=None):
    return lax.dot_general(
        a, b, (((0,), (0,)), ((), ())), preferred_element_type=F32, precision=precision
    )


def near(index, size, step):
    return lax.rem(index + (step + size), size)


def front_kernel(
    sizes, per, scale, cross_scale, gate_ref, left_ref, right_ref, omega_hbm,
    mine_ref, early_ref, late_ref, cross_ref,
    theta_ref, all_left, all_right, all_omega, bond_ref,
    part_ref, pair_ref, relay_ref, got_ref, held_ref,
    ya_ref, ya_relay, ya_got, xa_ref, xa_relay, xa_got,
    xb_ref, xb_relay, xb_got, yb_ref, yb_relay, yb_got,
    local, send, recv,
):
    ny, nx, nz, nc = sizes
    groups = nz * nc
    y, x, z, c = (lax.axis_index(a) for a in ("row", "x", "z", "core"))
    zc = z * nc + c
    twin = (y, x, z, 1 - c)
    part = left_ref.shape[0]
    rows = all_left.shape[3]
    bond_y, width = right_ref.shape
    step = omega_hbm.shape[0]
    band = rows // groups
    moves = []

    def push(src, dst, to):
        at = len(moves)
        move = pltpu.make_async_remote_copy(
            src_ref=src, dst_ref=dst, send_sem=send.at[at], recv_sem=recv.at[at],
            device_id=to, device_id_type=pl.DeviceIdType.MESH,
        )
        moves.append(move)
        return move

    def beside(axis, way):
        place = [y, x, z, c]
        place[axis] = near(place[axis], sizes[axis], way)
        return tuple(place)

    class Gather:
        def __init__(self, axis, block):
            me = (y, x, z)[axis]
            self.below, self.above = near(me, 4, -1), near(me, 4, 1)
            up, down = beside(axis, 1), beside(axis, -1)
            own = block(me, None)
            self.up, self.down = push(own, own, up), push(own, own, down)
            first, second = block(self.below, 0), block(self.above, 1)
            self.far_up, self.far_down = push(first, first, up), push(second, second, down)

        def start(self):
            self.up.start()
            self.down.start()

        def relay(self):
            self.up.wait_recv()
            self.far_up.start()
            self.down.wait_recv()
            self.far_down.start()

        def finish(self):
            self.far_up.wait_recv()
            self.far_down.wait_recv()

    class Reduce:
        def __init__(self, axis, block, relay, got):
            me = (y, x, z)[axis]
            up, down = beside(axis, 1), beside(axis, -1)
            far, above, below = near(me, 4, 2), near(me, 4, 1), near(me, 4, -1)
            self.block, self.me, self.above, self.below, self.far = block, me, above, below, far
            self.relay, self.got = relay, got
            self.far_up = push(block(far, 0), relay.at[0], up)
            self.far_down = push(block(far, 1), relay.at[1], down)
            self.up = push(block(above, None), got.at[0], up)
            self.down = push(block(below, None), got.at[1], down)

        def start(self):
            self.far_up.start()
            self.far_down.start()

        def middle(self):
            self.far_up.wait_recv()
            self.block(self.above, 0)[...] += self.relay[0]
            self.up.start()
            self.far_down.wait_recv()
            self.block(self.below, 1)[...] += self.relay[1]
            self.down.start()

        def finish(self):
            self.up.wait_recv()
            self.down.wait_recv()
            return self.block(self.me, None)[...] + self.got[0] + self.got[1]

    def halved(ref, rows_of, half):
        return ref if half is None else ref.at[pl.ds(half * (rows_of // 2), rows_of // 2)]

    def right_y(slot, half):
        size = bond_y if half is None else bond_y // 2
        begin = slot * bond_y + (0 if half is None else half * size)
        return all_right.at[x, pl.ds(pl.multiple_of(begin, 128), size), :]

    own_omega = [
        pltpu.make_async_copy(
            omega_hbm.at[:, pl.ds(pl.multiple_of((q * groups + zc) * width, width), width)],
            all_omega.at[y, :, pl.ds(q * width, width)], local.at[q],
        )
        for q in range(nx)
    ]
    for move in own_omega:
        move.start()
    all_right[x, pl.ds(pl.multiple_of(y * bond_y, bond_y), bond_y), :] = right_ref[...]
    by_y = Gather(0, right_y)
    by_y.start()
    across = []
    for dx in range(1, nx):
        to_x = near(x, nx, dx)
        src = left_ref.at[:, pl.ds(pl.multiple_of(to_x * rows, rows), rows)]
        across.append(push(src, all_left.at[zc, x], (y, to_x, z, c)))
    for move in across:
        move.start()
    all_left[zc, x] = left_ref[:, pl.ds(pl.multiple_of(x * rows, rows), rows)]

    def right_x(row):
        at = pl.ds(pl.multiple_of(row * bond_y, bond_y), bond_y)

        def block(slot, half):
            if half is None:
                return all_right.at[slot, at, :]
            size = bond_y // 2
            return all_right.at[slot, pl.ds(pl.multiple_of(row * bond_y + half * size, size), size), :]

        return Gather(1, block)

    by_x = [right_x(near(y, ny, d)) for d in (0, -1, 1, 2)]
    by_x[0].start()
    by_y.up.wait_recv()
    by_y.far_up.start()
    by_x[1].start()
    by_y.down.wait_recv()
    by_y.far_down.start()
    by_x[2].start()
    for move in own_omega:
        move.wait()
    omega_y = Gather(0, lambda slot, half: halved(all_omega.at[slot], step, half))
    omega_y.start()
    for move in across:
        move.wait_recv()
    left_z = Gather(2, lambda slot, half: halved(all_left.at[slot * nc + c], nx, half))
    left_z.start()
    left_twin = [push(all_left.at[near(z, nz, d) * nc + c], all_left.at[near(z, nz, d) * nc + c], twin)
                 for d in (0, -1, 1, 2)]
    left_twin[0].start()
    by_x[0].relay()
    by_y.finish()
    by_x[3].start()
    left_z.relay()
    left_twin[1].start()
    left_twin[2].start()
    by_x[1].relay()
    by_x[2].relay()
    left_z.finish()
    left_twin[3].start()
    by_x[3].relay()
    omega_y.relay()
    for move in left_twin:
        move.wait_recv()
    for xs in range(nx):
        for g in range(groups):
            at = (xs * groups + g) * part
            bond_ref[at : at + part, :] = all_left[g, xs]
    for ring in by_x:
        ring.finish()

    left = bond_ref[...]
    row_odd = lax.broadcasted_iota(jnp.int32, (rows, width), 0) % 2 == 1
    col_odd = lax.broadcasted_iota(jnp.int32, (rows, width), 1) % 2 == 1

    def coupling(row_flip, col_flip):
        def entry(s1, s2):
            a, b = s1 ^ row_flip, s2 ^ col_flip
            return gate_ref[2 * s1 + s2, 2 * a + b]

        even = jnp.where(col_odd, entry(0, 1), entry(0, 0))
        odd = jnp.where(col_odd, entry(1, 1), entry(1, 0))
        return jnp.where(row_odd, odd, even)

    for xs in range(nx):
        bare = tdot(left, all_right[xs])
        row_partner = jnp.where(row_odd, pltpu.roll(bare, 1, 0), pltpu.roll(bare, rows - 1, 0))

        def col_partner(v):
            return jnp.where(col_odd, pltpu.roll(v, 1, 1), pltpu.roll(v, width - 1, 1))

        mixed = (coupling(0, 0) * bare + coupling(0, 1) * col_partner(bare)) + (
            coupling(1, 0) * row_partner + coupling(1, 1) * col_partner(row_partner)
        )
        theta_ref[:, xs * width : (xs + 1) * width] = mixed.astype(BF16)
    omega_y.finish()
    theta = theta_ref[...]
    for q in range(ny):
        value = lax.dot_general(
            theta, all_omega[q], (((1,), (1,)), ((), ())), preferred_element_type=F32
        )
        part_ref[:, :, q * step : (q + 1) * step] = value.reshape(groups, band, step)

    order = (2, 1, -1, 0)
    pairs = [
        push(part_ref.at[near(z, nz, d) * nc + 1 - c], pair_ref.at[q], twin) for q, d in enumerate(order)
    ]
    for move in pairs:
        move.start()

    def block_z(slot, half):
        return halved(part_ref.at[slot * nc + c], band, half)

    def add_pair(q):
        pairs[q].wait_recv()
        part_ref[near(z, nz, order[q]) * nc + c] += pair_ref[q]

    sum_z = Reduce(2, block_z, relay_ref, got_ref)
    add_pair(0)
    sum_z.start()
    add_pair(1)
    add_pair(2)
    sum_z.middle()
    add_pair(3)
    total = sum_z.finish()
    held_ref[zc] = total

    rows_z = Gather(2, lambda slot, half: halved(held_ref.at[slot * nc + c], band, half))
    rows_z.start()
    rows_twin = [push(held_ref.at[near(z, nz, d) * nc + c], held_ref.at[near(z, nz, d) * nc + c], twin)
                 for d in (0, -1, 1, 2)]
    rows_twin[0].start()
    mine_ref[...] = total
    rows_z.relay()
    rows_twin[1].start()
    rows_twin[2].start()
    rows_z.finish()
    rows_twin[3].start()
    for move in rows_twin:
        move.wait_recv()
    k = mine_ref.shape[1]
    nt = k // TILE
    piece = early_ref.shape[5]

    def columns(at, count=TILE):
        return held_ref[:, :, pl.ds(at, count)].reshape(rows, count)

    def tiles(half, out):
        low, high = tile_halves(nt)[half]
        starts = [0]
        for i in range(low, high):
            starts.append(starts[-1] + nt - i)

        def tile(t, carry):
            at = jnp.minimum(zc * per + t, starts[-1] - 1)
            row, begin = jnp.int32(low), jnp.int32(0)
            for q in range(1, len(starts) - 1):
                row = jnp.where(at >= starts[q], low + q, row)
                begin = jnp.where(at >= starts[q], starts[q], begin)
            i = pl.multiple_of(row * TILE, TILE)
            j = pl.multiple_of((row + at - begin) * TILE, TILE)
            value = tdot(columns(i), columns(j), HI) * scale
            for q in range(ny):
                for r in range(nx):
                    at = (q * nx + r) * piece
                    spot = (q, r) if half == 0 else (r, q)
                    out[spot[0], spot[1], pl.ds(t, 1)] = value[at : at + piece].reshape(1, piece, TILE)
            return carry

        lax.fori_loop(0, per, tile, 0)

    def lower_rows(ref, slot, half):
        if half is None:
            return ref.at[slot]
        return ref.at[slot, :, pl.ds(half * (piece // 2), piece // 2)]

    first_a = Reduce(0, lambda s, h: halved(ya_ref.at[s], nx, h), ya_relay, ya_got)
    first_b = Reduce(1, lambda s, h: halved(xb_ref.at[s], ny, h), xb_relay, xb_got)
    tiles(0, ya_ref)
    first_a.start()
    tiles(1, xb_ref)
    first_a.middle()
    first_b.start()
    xa_ref[...] = first_a.finish()
    then_a = Reduce(1, lambda s, h: lower_rows(xa_ref, s, h), xa_relay, xa_got)
    then_a.start()
    first_b.middle()
    then_a.middle()
    yb_ref[...] = first_b.finish()
    then_b = Reduce(0, lambda s, h: lower_rows(yb_ref, s, h), yb_relay, yb_got)
    then_b.start()
    early_ref[y, x, z, c] = then_a.finish()

    spots = ((2, 0, 1), (0, 1, 2), (1, 2, 0))
    here = (y, x, z)

    def plane(t, phase):
        axes = spots[t]
        along = axes[phase]

        def block(slot, half):
            index = [here[0], here[1], here[2]]
            for done in axes[:phase]:
                index[done] = slice(None)
            index[along] = slot
            if half is not None and phase == 0:
                rows_at = pl.ds(half * (piece // 2), piece // 2)
                return early_ref.at[index[0], index[1], index[2], c, t, rows_at]
            if half is not None:
                index[axes[0]] = pl.ds(2 * half, 2)
            return early_ref.at[index[0], index[1], index[2], c, t]

        return along, block

    rings = []
    for t in range(per):
        along, block = plane(t, 0)
        rings.append(Gather(along, block))
        rings[t].start()
    then_b.middle()
    for ring in rings:
        ring.relay()
    late_ref[...] = then_b.finish()
    second = []
    for t in range(per):
        rings[t].finish()
        along, block = plane(t, 1)
        second.append(Gather(along, block))
        second[t].start()
    for ring in second:
        ring.relay()
    third, to_twin = [], []
    for t in range(per):
        second[t].finish()
        along, block = plane(t, 2)
        third.append(Gather(along, block))
        third[t].start()
        me = here[along]
        group = []
        for d in (0, -1, 1, 2):
            ref = block(near(me, 4, d), None)
            group.append(push(ref, ref, twin))
        to_twin.append(group)
        group[0].start()

    theta = theta_ref[...]
    for at in range(0, k, TILE):
        head, rest = split(columns(at))
        value = (tdot(head, theta) + tdot(rest, theta)) * cross_scale
        for q in range(nx):
            cross_ref[q, at : at + TILE, :] = value[:, q * width : (q + 1) * width]

    for t in range(per):
        third[t].relay()
        to_twin[t][1].start()
        to_twin[t][2].start()
    for t in range(per):
        third[t].finish()
        to_twin[t][3].start()
    for group in to_twin:
        for move in group:
            move.wait_recv()
    for move in moves:
        move.wait_send()


def front(gate, left, right, omega, sizes, per, scale, cross_scale):
    ny, nx, nz, nc = sizes
    groups, chunks = nz * nc, ny * nx
    part, rows = left.shape[0], left.shape[1] // nx
    bond_y, width = right.shape
    step = omega.shape[0]
    k, cols, band = ny * step, nx * width, rows // groups
    piece = TILE // chunks
    smem = pl.BlockSpec(memory_space=pltpu.SMEM)
    dma = pltpu.SemaphoreType.DMA
    vmem = pltpu.VMEM

    def sums(first, second):
        return [
            vmem((first, second, per, piece, TILE), F32),
            vmem((2, second // 2, per, piece, TILE), F32),
            vmem((2, second, per, piece, TILE), F32),
            vmem((second, per, piece, TILE), F32),
            vmem((2, per, piece // 2, TILE), F32),
            vmem((2, per, piece, TILE), F32),
        ]

    return pl.pallas_call(
        functools.partial(front_kernel, sizes, per, scale, cross_scale),
        out_shape=(
            jax.ShapeDtypeStruct((band, k), F32),
            jax.ShapeDtypeStruct((ny, nx, nz, nc, per, piece, TILE), F32),
            jax.ShapeDtypeStruct((per, piece, TILE), F32),
            jax.ShapeDtypeStruct((nx, k, width), F32),
        ),
        in_specs=[smem, WHOLE, WHOLE, pl.BlockSpec(memory_space=pl.ANY)],
        out_specs=(WHOLE,) * 4,
        scratch_shapes=[
            vmem((rows, cols), BF16),
            vmem((groups, nx, part, rows), BF16),
            vmem((nx, bond_y * ny, width), BF16),
            vmem((ny, step, cols), BF16),
            vmem((bond_y * ny, rows), BF16),
            vmem((groups, band, k), F32),
            vmem((nz, band, k), F32),
            vmem((2, band // 2, k), F32),
            vmem((2, band, k), F32),
            vmem((groups, band, k), F32),
        ]
        + sums(ny, nx)
        + sums(nx, ny)
        + [dma((nx,)), dma((128,)), dma((128,))],
        compiler_params=pltpu.CompilerParams(vmem_limit_bytes=VMEM_LIMIT, has_side_effects=True),
        name="front",
    )(gate, left, right, omega)


def leaf(rows, task=None, tasks=0):
    lane = lax.broadcasted_iota(jnp.int32, (8, HALF), 1)
    sub = lax.broadcasted_iota(jnp.int32, (8, HALF), 0)
    rows = list(rows)
    count = len(rows)
    done = []
    for j in range(count):
        base = 8 * j
        here = (lane >= base) & (lane < base + 8)
        part = rows[j]
        cols = [jnp.broadcast_to(part[:, base + k : base + k + 1], (8, HALF)) for k in range(8)]
        part = jnp.where(here, jnp.where(lane - base == sub, 1.0, 0.0), part)
        tri = jnp.zeros((8, HALF), F32)
        for k in range(8):
            at = sub == k
            pivot = jnp.broadcast_to(cols[k][k : k + 1, :], (8, HALF))
            inv = 1.0 / pivot
            row = jnp.broadcast_to(part[k : k + 1, :], (8, HALF))
            tri = jnp.where(at, row * lax.rsqrt(pivot), tri)
            factor = cols[k] * inv
            part = jnp.where(at, row * inv, part - factor * row)
            for m in range(k + 1, 8):
                mrow = jnp.broadcast_to(cols[m][k : k + 1, :], (8, HALF))
                cols[m] = jnp.where(at, mrow * inv, cols[m] - factor * mrow)
        done.append(jnp.where(lane < base + 8, tri, 0.0))
        for extra in range(j * tasks // count, (j + 1) * tasks // count):
            task(extra)
        if j + 1 < count:
            prow = [jnp.broadcast_to(part[k : k + 1, :], (8, HALF)) for k in range(8)]
            for i in range(j + 1, count):
                mine = rows[i]
                terms = [
                    jnp.broadcast_to(mine[:, base + k : base + k + 1], (8, HALF)) * prow[k]
                    for k in range(8)
                ]
                while len(terms) > 1:
                    terms = [terms[q] + terms[q + 1] for q in range(0, len(terms), 2)]
                rows[i] = jnp.where(here, 0.0, mine) - terms[0]
    return done


def stage_kernel(plan, per, *refs):
    first, stop, nt, chunks, has_carry, has_tiles = plan
    refs = list(refs)
    g_ref = refs.pop(0) if has_tiles else None
    carry_ref = refs.pop(0) if has_carry else None
    uh_ref, ul_ref, inv_ref = refs[:3]
    refs = refs[3:]
    last = stop == nt
    out_ref = None if last else refs.pop(0)
    grid_ref, a_ref, l_ref, uab_ref, s3_ref, t3_ref, sem = refs[:7]
    extra_ref = refs[7] if has_carry and has_tiles else None
    m = (nt - first) * TILE
    size = nt - first
    count = stop - first
    t_ref = grid_ref.reshape(m, m)
    copies = []
    if has_tiles:
        groups = g_ref.shape[0] // chunks
        source = g_ref.reshape(chunks, groups, per, TILE // chunks, TILE)
        target = grid_ref if extra_ref is None else extra_ref
        low, high = (first, stop) if not has_carry else (first, nt)
        for at, (i, j) in enumerate((i, j) for i in range(low, high) for j in range(i, nt)):
            rows = pl.ds((i - first) * chunks, chunks)
            cols = pl.ds((j - first) * TILE, TILE)
            copies.append(
                pltpu.make_async_copy(
                    source.at[:, at // per, at % per], target.at[rows, :, cols], sem.at[0]
                )
            )
    if has_carry:
        for i in range(size):
            at = pl.ds(i * TILE, TILE)
            cols = pl.ds(i * TILE, m - i * TILE)
            copies.append(pltpu.make_async_copy(carry_ref.at[at, cols], t_ref.at[at, cols], sem.at[1]))
    for copy in copies:
        copy.start()
    if not has_carry and not last:
        t_ref[count * TILE :, count * TILE :] = jnp.zeros((m - count * TILE,) * 2, F32)
    for copy in copies:
        copy.wait()
    if extra_ref is not None:
        e_ref = extra_ref.reshape(m, m)

        def add_row(r, carry):
            rat = pl.multiple_of(r * TILE, TILE)

            def add(c, carry):
                cat = pl.multiple_of(c * TILE, TILE)
                t_ref[pl.ds(rat, TILE), pl.ds(cat, TILE)] += e_ref[pl.ds(rat, TILE), pl.ds(cat, TILE)]
                return carry

            return lax.fori_loop(r, size, add, carry)

        lax.fori_loop(0, size, add_row, 0)

    def in_row(r):
        return (size - r + 1) // 2

    def total_tasks(p):
        left = size - 1 - p
        pairs = left // 2
        count = jnp.where(left % 2 == 0, pairs * (pairs + 1), (pairs + 1) * (pairs + 1)) - 1
        return jnp.where((p < 0) | (left < 1), 0, count)

    def apply(r, q):
        rat = pl.multiple_of(r * TILE, TILE)
        cat = pl.multiple_of((size - 2 - 2 * q) * TILE, TILE)
        t_ref[pl.ds(rat, TILE), pl.ds(cat, 2 * TILE)] -= jnp.dot(
            t3_ref[pl.ds(rat, TILE), :], s3_ref[:, pl.ds(cat, 2 * TILE)], preferred_element_type=F32
        )

    def update(p, at):
        row, begin, start = p + 1, jnp.int32(0), in_row(p + 1) - 1
        for _ in range(size - 2):
            nxt = at >= start
            begin = jnp.where(nxt, start, begin)
            row = jnp.where(nxt, row + 1, row)
            start = jnp.where(nxt, start + in_row(row), start)
        apply(row, at - begin)

    def half(p, h, carry):
        base = pl.multiple_of(p * TILE, TILE)
        mid = pl.multiple_of(p * TILE + HALF, HALF)

        @pl.when(h == 0)
        def _():
            a_ref[...] = t_ref[pl.ds(base, HALF), pl.ds(base, HALF)]

        @pl.when(h == 1)
        def _():
            a_ref[...] = t_ref[pl.ds(mid, HALF), pl.ds(mid, HALF)] - tdot(uab_ref[...], uab_ref[...], HI)

        done = carry
        busy = done + TASKS <= total_tasks(p - 1) if size > 4 else False

        def factor(task=None, tasks=0):
            out = leaf([a_ref[8 * i : 8 * i + 8, :] for i in range(HALF // 8)], task, tasks)
            for i, rows in enumerate(out):
                l_ref[8 * i : 8 * i + 8, :] = rows

        if size > 4:

            @pl.when(busy)
            def _():
                factor(lambda extra: update(p - 1, done + extra), TASKS)

            @pl.when(jnp.logical_not(busy))
            def _():
                factor()

        else:
            factor()

        @pl.when(h == 0)
        def _():
            inv_ref[p, 0:HALF, 0:HALF] = l_ref[...]
            inv_ref[p, 0:HALF, HALF:] = jnp.zeros((HALF, HALF), F32)
            uab_ref[...] = jnp.dot(
                l_ref[...], t_ref[pl.ds(base, HALF), pl.ds(mid, HALF)], precision=HI
            )

        @pl.when(h == 1)
        def _():
            cross = tdot(uab_ref[...], inv_ref[p, 0:HALF, 0:HALF], HI)
            inv_ref[p, HALF:, 0:HALF] = -jnp.dot(l_ref[...], cross, precision=HI)
            inv_ref[p, HALF:, HALF:] = l_ref[...]

        return jnp.where(busy, done + TASKS, done)

    def panel(p, carry):
        base = pl.multiple_of(p * TILE, TILE)
        done = lax.fori_loop(0, 2, functools.partial(half, p), jnp.int32(0))

        def rest(at, carry):
            update(p - 1, at)
            return carry

        lax.fori_loop(done, total_tasks(p - 1), rest, 0)

        def row_tile(c, carry):
            at = pl.multiple_of(c * TILE, TILE)
            u = jnp.dot(inv_ref[p], t_ref[pl.ds(base, TILE), pl.ds(at, TILE)], precision=HI)
            head, rest = split(u)
            uh_ref[pl.ds(base, TILE), pl.ds(at, TILE)] = head
            ul_ref[pl.ds(base, TILE), pl.ds(at, TILE)] = rest
            for third, value in enumerate((head, rest, head)):
                s3_ref[third * TILE : (third + 1) * TILE, pl.ds(at, TILE)] = value
            for third, value in enumerate((head.T, head.T, rest.T)):
                t3_ref[pl.ds(at, TILE), third * TILE : (third + 1) * TILE] = value
            return carry

        lax.fori_loop(p + 1, size, row_tile, 0)

        @pl.when(p + 1 < size)
        def _():
            apply(p + 1, in_row(p + 1) - 1)

        return carry

    lax.fori_loop(0, count, panel, 0)
    if not last:

        def rest(at, carry):
            update(count - 1, at)
            return carry

        lax.fori_loop(0, total_tasks(count - 1), rest, 0)
    if out_ref is not None:
        back = []
        for i in range(count, size):
            at = pl.ds((i - count) * TILE, TILE)
            cols = pl.ds((i - count) * TILE, m - i * TILE)
            mine = t_ref.at[pl.ds(i * TILE, TILE), pl.ds(i * TILE, m - i * TILE)]
            back.append(pltpu.make_async_copy(mine, out_ref.at[at, cols], sem.at[0]))
        for copy in back:
            copy.start()
        for copy in back:
            copy.wait()


def stage(first, stop, n, per, chunks, tiles=None, carry=None):
    nt = n // TILE
    m = n - first * TILE
    rows = (stop - first) * TILE
    piece = TILE // chunks
    args = [v for v in (tiles, carry) if v is not None]
    out_shape = [
        jax.ShapeDtypeStruct((rows, m), BF16),
        jax.ShapeDtypeStruct((rows, m), BF16),
        jax.ShapeDtypeStruct((stop - first, TILE, TILE), F32),
    ]
    out_specs = [WHOLE] * 3
    if stop < nt:
        out_shape.append(jax.ShapeDtypeStruct((m - rows, m - rows), F32))
        out_specs.append(pl.BlockSpec(memory_space=pl.ANY))
    scratch = [
        pltpu.VMEM((m // piece, piece, m), F32),
        pltpu.VMEM((HALF, HALF), F32),
        pltpu.VMEM((HALF, HALF), F32),
        pltpu.VMEM((HALF, HALF), F32),
        pltpu.VMEM((3 * TILE, m), BF16),
        pltpu.VMEM((m, 3 * TILE), BF16),
        pltpu.SemaphoreType.DMA((2,)),
    ]
    if len(args) == 2:
        scratch.append(pltpu.VMEM((m // piece, piece, m), F32))
    plan = (first, stop, nt, chunks, carry is not None, tiles is not None)
    return pl.pallas_call(
        functools.partial(stage_kernel, plan, per),
        out_shape=tuple(out_shape),
        in_specs=[pl.BlockSpec(memory_space=pl.ANY)] * len(args),
        out_specs=tuple(out_specs),
        scratch_shapes=scratch,
        compiler_params=pltpu.CompilerParams(vmem_limit_bytes=VMEM_LIMIT),
        cost_estimate=pl.CostEstimate(
            flops=40 * 10**9, bytes_accessed=rows * m * 8, transcendentals=0
        ),
    )(*args)


def solve_kernel(plan, *refs):
    stages = len(plan)
    factors = refs[: 3 * stages]
    s_ref, w_ref, basis_ref, proj_ref, y_ref = refs[3 * stages : 3 * stages + 5]
    held = refs[3 * stages + 5 : 6 * stages + 5]
    sem = refs[6 * stages + 5]
    copies = [
        pltpu.make_async_copy(a, b, sem.at[q]) for q, (a, b) in enumerate(zip(factors, held))
    ]
    for copy in copies:
        copy.start()
    mine, n = s_ref.shape
    nt = n // TILE
    padded = jnp.concatenate([s_ref[...], jnp.zeros((HALF - mine, n), F32)], axis=0)
    y_ref[:, :HALF] = padded.T
    y_ref[:, HALF:] = w_ref[...]
    for q, (first, stop) in enumerate(plan):
        uh_ref, ul_ref, inv_ref = held[3 * q : 3 * q + 3]
        for copy in copies[3 * q : 3 * q + 3]:
            copy.wait()
        for p in range(first, stop):
            rows = slice(p * TILE, (p + 1) * TILE)
            local = slice((p - first) * TILE, (p - first + 1) * TILE)
            y = jnp.dot(inv_ref[p - first], y_ref[rows, :], precision=HI)
            y_ref[rows, :] = y
            head, rest = split(y)

            def tail(r, carry):
                at = pl.multiple_of(r * TILE, TILE)
                here = pl.multiple_of((r - first) * TILE, TILE)
                uh = uh_ref[local, pl.ds(here, TILE)]
                ul = ul_ref[local, pl.ds(here, TILE)]
                y_ref[pl.ds(at, TILE), :] -= tdot(uh, head) + (tdot(uh, rest) + tdot(ul, head))
                return carry

            lax.fori_loop(p + 1, nt, tail, 0)
    basis_ref[...] = y_ref[:, :HALF].T[:mine]
    block = proj_ref.shape[0]
    at = pl.multiple_of(lax.axis_index("row") * block, block)
    proj_ref[...] = y_ref[pl.ds(at, block), HALF:]


def solve(plan, factors, sketch, weights):
    mine, n = sketch.shape
    flat = [v for part in factors for v in part]
    return pl.pallas_call(
        functools.partial(solve_kernel, plan),
        out_shape=(jax.ShapeDtypeStruct((mine, n), F32), jax.ShapeDtypeStruct((n // lax.axis_size("row"), HALF), F32)),
        in_specs=[pl.BlockSpec(memory_space=pl.ANY)] * len(flat) + [WHOLE, WHOLE],
        out_specs=(WHOLE, WHOLE),
        scratch_shapes=[pltpu.VMEM((n, 2 * HALF), F32)]
        + [pltpu.VMEM(v.shape, v.dtype) for v in flat]
        + [pltpu.SemaphoreType.DMA((len(flat),))],
        compiler_params=pltpu.CompilerParams(vmem_limit_bytes=VMEM_LIMIT),
        name="solve",
    )(*flat, sketch, weights)


CUTS = ((0, 3), (3, 6), (6, 9))


def tile_halves(nt):
    cut = CUTS[0][1]
    return (0, cut), (cut, nt)


def tiles_each(nt, groups):
    counts = [sum(nt - i for i in range(low, high)) for low, high in tile_halves(nt)]
    return -(-max(counts) // groups)


def on_device(left_site, right_site, gate, omega):
    sizes = tuple(lax.axis_size(a) for a in ("row", "x", "z", "core"))
    ny, nx, nz, nc = sizes
    total = left_site.shape[0] * ny
    width = right_site.shape[1]
    n = omega.shape[1] * ny
    chunks = ny * nx
    per = tiles_each(n // TILE, nz * nc)
    sketch, early, late, weights = front(
        gate, left_site.T, right_site, omega.T, sizes, per, 1.0 / total, 1.0 / math_sqrt(total)
    )
    early = early.reshape((ny * nx * nz * nc,) + early.shape[4:])
    late = lax.all_gather(late[None], ("row", "x", "z", "core"), axis=0, tiled=True)
    weights = lax.psum_scatter(weights, "x", scatter_dimension=0, tiled=True)

    *part_a, carry = stage(*CUTS[0], n, per, chunks, tiles=early)
    *part_b, carry = stage(*CUTS[1], n, per, chunks, tiles=late, carry=carry)
    carry, weights = lax.optimization_barrier((carry, weights))
    weights = lax.psum(weights, "row").reshape(n, width)
    part_c = stage(*CUTS[2], n, per, chunks, carry=carry)
    basis, projected = solve(CUTS, (part_a, part_b, part_c), sketch, weights)
    return basis, projected


def math_sqrt(value):
    return float(np.sqrt(value))


def solution(mesh):
    fine = Mesh(mesh.devices.reshape(4, 4, 4, 2), ("row", "x", "z", "core"))
    col = ("x", "z", "core")
    in_specs = (P("row", col), P("row", col), P(), P(None, "row"))
    out_specs = (P(("row",) + col, None), P("row", col))
    return jax.shard_map(
        on_device, mesh=fine, in_specs=in_specs, out_specs=out_specs, check_vma=False
    )
```
